512 devices in a mesh: space: 32 (over z, x_lo), chan: 16 (over x_hi, y, core).
Axes of the slice: x: 4 (x_hi: 2, x_lo: 2; x = x_hi * 2 + x_lo), y: 4, z: 16, core: 2. Of those that a mesh axis runs over, the one named last changes fastest.
Arguments:
- volume: bfloat16 [64, 256, 8, 128], P('space', 'chan'), may hold values from -6 to 6
- kernel: bfloat16 [27, 256, 256], P(None, 'chan'), may hold values from -0.078125 to 0.078125
- cotangent: bfloat16 [64, 256, 8, 128], P('space', 'chan'), may hold values from -6 to 6
Outputs:
- output_map: bfloat16 [64, 256, 8, 128], P('space', 'chan')
- input_grad: bfloat16 [64, 256, 8, 128], P('space', 'chan')
- kernel_grad: float32 [27, 256, 256], P(None, 'chan')
The draws below stay inside these ranges and needn't reach their ends.
All inputs are finite; a program needn't handle non-finite values.
Results may differ from the reference program's by a relative error of at most 0.001.
Values may be sent and summed in bfloat16 or wider, within the bound.
A program may use at most 128 MiB of HBM per device.

```python
import math
import jax
import jax.numpy as jnp
from jax import lax

C = 256
F = 256
H = 8
W = 128
NZ = 64


def shard_levels(stream_key, extent, shards, low, high):
    gain, own = 1.0, jax.random.fold_in(stream_key, 6)
    for axis_at, parts in shards:
        steps = jnp.exp(jax.random.uniform(jax.random.fold_in(own, axis_at), (parts,), jnp.float32, low / len(shards), high / len(shards)))
        gain = gain * jnp.repeat(steps, extent[axis_at] // parts).reshape([-1 if axis == axis_at else 1 for axis in range(len(extent))])
    return gain


def centred(own_key, dims, deviation, bound, split=(), kind=jnp.bfloat16):
    gain = shard_levels(own_key, dims, split, -0.22, 0.18) if split else 1.0
    drawn = jax.random.normal(own_key, dims, jnp.float32) * deviation * gain
    return jnp.minimum(jnp.maximum(drawn, -bound), bound).astype(kind)


def setup_inputs(seed: int = 0) -> dict:
    splits = jax.random.split(jax.random.key(seed), 4)
    volume = centred(splits[0], (NZ, C, H, W), 1.0, 6.0, ((0, 32), (1, 16)))
    kernel = centred(splits[1], (27, F, C), (27 * C) ** -0.5, 0.078125, ((1, 16),))
    cotangent = centred(splits[2], (NZ, F, H, W), 1.0, 6.0, ((0, 32), (1, 16)))
    return dict(volume=volume, kernel=kernel, cotangent=cotangent)


def pad_cells(block):
    return jnp.pad(block, ((1, 1), (0, 0), (1, 1), (1, 1)))

def reference(volume, kernel, cotangent):
    volume_full = volume.astype(jnp.float32)
    grad_full = cotangent.astype(jnp.float32)
    kernel_full = kernel.astype(jnp.float32)
    volume_pad = pad_cells(volume_full)
    grad_pad = pad_cells(grad_full)
    output_sum = jnp.zeros((NZ, F, H, W), jnp.float32)
    input_sum = jnp.zeros((NZ, C, H, W), jnp.float32)
    kernel_terms = []
    for tap_index in range(27):
        depth_step = tap_index // 9
        row_step = tap_index // 3 % 3
        col_step = tap_index % 3
        window = volume_pad[depth_step:depth_step + NZ, :, row_step:row_step + H, col_step:col_step + W]
        output_sum = output_sum + jnp.einsum('fc,zchw->zfhw', kernel_full[tap_index], window, precision=lax.Precision.HIGHEST)
        kernel_terms.append(jnp.einsum('zfhw,zchw->fc', grad_full, window, precision=lax.Precision.HIGHEST))
        back_window = grad_pad[2 - depth_step:2 - depth_step + NZ, :, 2 - row_step:2 - row_step + H, 2 - col_step:2 - col_step + W]
        input_sum = input_sum + jnp.einsum('fc,zfhw->zchw', kernel_full[tap_index], back_window, precision=lax.Precision.HIGHEST)
    scale_factor = 1.0 / math.sqrt(NZ * H * W)
    kernel_grad = jnp.stack(kernel_terms) * scale_factor
    return (output_sum.astype(jnp.bfloat16), input_sum.astype(jnp.bfloat16), kernel_grad)
```

```python
import functools
import math

import jax
import jax.numpy as jnp
from jax import lax
from jax.experimental import pallas as pl
from jax.experimental.pallas import tpu as pltpu
from jax.sharding import PartitionSpec as P

MESH = pl.DeviceIdType.MESH
COPIES = 96


def col_shift(x, step, column):
    if step == 0:
        return x
    width = x.shape[1]
    if step == 1:
        moved = pltpu.roll(x, width - 1, 1)
        return jnp.where(column == 127, 0.0, moved)
    moved = pltpu.roll(x, 1, 1)
    return jnp.where(column == 0, 0.0, moved)


def row_shift(x, step):
    if step == 0:
        return x
    zeros = jnp.zeros((x.shape[0], 128), x.dtype)
    if step == 1:
        return jnp.concatenate([x[:, 128:], zeros], axis=1)
    return jnp.concatenate([zeros, x[:, :-128]], axis=1)


def tap_sum(sums_ref, sign, column):
    total = None
    for b in range(3):
        line = None
        for c in range(3):
            tap = 3 * b + c
            part = col_shift(sums_ref[16 * tap : 16 * tap + 16, :], sign * (c - 1), column)
            line = part if line is None else line + part
        moved = row_shift(line, sign * (b - 1))
        total = moved if total is None else total + moved
    return total


def layer_kernel(
    nspace,
    scale,
    vol_ref,
    cot_ref,
    ker_ref,
    kt_ref,
    out_ref,
    inp_ref,
    grad_ref,
    vg,
    cg,
    wr,
    cs,
    sums,
    part,
    near,
    quad,
    far,
    own,
    full,
    send_sem,
    recv_sem,
):
    s = lax.axis_index("space")
    c = lax.axis_index("chan")
    nz = nspace // 2
    z, x_lo = s // 2, s % 2
    x_hi, y, core = c // 8, (c // 2) % 4, c % 2
    flip = (1 - x_hi) * 8 + y * 2 + core
    mate = c + 1 - 2 * core

    def at(dz, same):
        zz = lax.rem(z + dz + nz, nz)
        xx = x_lo if same else 1 - x_lo
        return zz * 2 + xx

    pair = at(0, False)
    edge = lax.rem(s + nspace + 2 * x_lo - 1, nspace)

    def chan_of(yy):
        return x_hi * 8 + lax.rem(y + yy, 4) * 2 + core

    peers = [(s, lax.rem(c + m, 16)) for m in range(1, 16)]
    peers += [(pair, c), (pair, flip), (edge, flip)]
    for dz in (1, -1, 2, -2):
        peers += [(at(dz, True), c), (at(dz, False), c)]
    peers += [(at(4, True), c), (at(-4, True), c), (at(8, True), c)]
    barrier = pltpu.get_barrier_semaphore()
    for peer in peers:
        pl.semaphore_signal(barrier, inc=1, device_id=peer, device_id_type=MESH)

    column = lax.broadcasted_iota(jnp.int32, (16, 1024), 1) % 128
    for plane in range(2):
        local = cot_ref[plane].astype(jnp.float32)
        for tap in range(9):
            b, cc = tap // 3, tap % 3
            moved = row_shift(col_shift(local, 1 - cc, column), 1 - b)
            cs[144 * plane + 16 * tap : 144 * plane + 16 * tap + 16, :] = moved.astype(jnp.bfloat16)
    vg[1:3, x_hi, y, core] = vol_ref[...]
    cg[1:3, x_hi, y, core] = cot_ref[...]
    wr[:, c] = kt_ref[c]
    pl.semaphore_wait(barrier, len(peers))

    count = [0]
    begun = []

    def send(src, dst, peer):
        at_sem = count[0]
        count[0] += 1
        copy = pltpu.make_async_remote_copy(
            src_ref=src,
            dst_ref=dst,
            send_sem=send_sem.at[at_sem],
            recv_sem=recv_sem.at[at_sem],
            device_id=peer,
            device_id_type=MESH,
        )
        copy.start()
        begun.append(copy)
        return copy

    pair_src, pair_dst = 1 - x_lo, 3 * x_lo
    edge_src, edge_dst = x_lo, 3 * (1 - x_lo)

    v1 = [send(vol_ref, vg.at[pl.ds(1, 2), x_hi, y, core], (s, flip))]
    for to in (c, flip):
        v1.append(send(vol_ref.at[edge_src], vg.at[edge_dst, x_hi, y, core], (edge, to)))
    for to in (c, flip):
        v1.append(send(vol_ref.at[pair_src], vg.at[pair_dst, x_hi, y, core], (pair, to)))
    c1 = [
        send(cot_ref, cg.at[pl.ds(1, 2), x_hi, y, core], (s, chan_of(yy))) for yy in (1, 3, 2)
    ]

    for copy in v1:
        copy.wait_recv()
    v2 = []
    for yy in (1, 3, 2):
        v2.append(send(vg.at[:, :, y, core], vg.at[:, :, y, core], (s, chan_of(yy))))
    v3 = [send(vg.at[:, :, y, core], vg.at[:, :, y, core], (s, mate))]

    for copy in c1:
        copy.wait_recv()
    c2 = [
        send(
            cg.at[pl.ds(1, 2), x_hi, :, core],
            cg.at[pl.ds(1, 2), x_hi, :, core],
            (s, flip),
        )
    ]
    for to in (c, flip):
        c2.append(
            send(cg.at[edge_src + 1, x_hi, :, core], cg.at[edge_dst, x_hi, :, core], (edge, to))
        )
    for to in (c, flip):
        c2.append(
            send(cg.at[pair_src + 1, x_hi, :, core], cg.at[pair_dst, x_hi, :, core], (pair, to))
        )
    w1 = []
    for m in range(1, 16):
        to = lax.rem(c + m, 16)
        w1.append(send(kt_ref.at[to], wr.at[:, c], (s, to)))

    for yy, copy in zip((3, 1, 2), v2):
        copy.wait_recv()
        from_y = lax.rem(y + yy, 4)
        v3.append(send(vg.at[:, :, from_y, core], vg.at[:, :, from_y, core], (s, mate)))
    for copy in v3:
        copy.wait_recv()

    low = s == 0
    high = s == nspace - 1

    def plane_of(ref, index):
        return ref[index].reshape(256, 1024)

    def cell_dot(lhs, plane):
        return lax.dot_general(
            lhs, plane, (((1,), (1,)), ((), ())), preferred_element_type=jnp.float32
        )

    zero_rows = jnp.zeros((144, 256), jnp.float32)
    first = cell_dot(cs[0:144, :], plane_of(vg, 0))
    second = cell_dot(cs[...], plane_of(vg, 1))
    third = cell_dot(cs[...], plane_of(vg, 2))
    fourth = cell_dot(cs[144:288, :], plane_of(vg, 3))
    first = jnp.where(low, zero_rows, first)
    fourth = jnp.where(high, zero_rows, fourth)
    part[0:9] = (first + second[144:288]).reshape(9, 16, 256)
    part[9:18] = (second[0:144] + third[144:288]).reshape(9, 16, 256)
    part[18:27] = (third[0:144] + fourth).reshape(9, 16, 256)
    part[27:32] = jnp.zeros((5, 16, 256), jnp.float32)

    r = z % 4
    n1 = []
    moves = [(1, True), (-1, True), (2, True), (1, False), (-1, False), (-2, False), (0, False)]
    for slot, (dz, same) in enumerate(moves):
        group = (x_lo if same else 1 - x_lo) * 4 + (r + dz + 4) % 4
        n1.append(send(part.at[pl.ds(group * 4, 4)], near.at[slot], (at(dz, same), c)))

    def conv(weights, ref, first_plane):
        rows = ref[first_plane : first_plane + 3].reshape(768, 1024)
        sums[...] = jnp.dot(weights, rows, preferred_element_type=jnp.float32)

    blank = jnp.zeros((144, 256), jnp.bfloat16)

    def edge_weights(taps, plane):
        below, middle, above = taps
        if plane == 0:
            below = jnp.where(low, blank, below)
        else:
            above = jnp.where(high, blank, above)
        return jnp.concatenate([below, middle, above], axis=1)

    forward = [ker_ref[9 * a : 9 * a + 9].reshape(144, 256) for a in range(3)]
    for plane in range(2):
        conv(edge_weights(forward, plane), vg, plane)
        out_ref[plane] = tap_sum(sums, 1, column).astype(jnp.bfloat16)

    for copy in c2:
        copy.wait_recv()
    c3 = send(cg.at[:, :, :, core], cg.at[:, :, :, core], (s, mate))

    for copy in n1:
        copy.wait_recv()
    zi = z // 4
    mine = x_lo * 4 + r
    total = part[pl.ds(mine * 4, 4)]
    for slot in range(7):
        total = total + near[slot]
    quad[...] = total
    f1 = []
    for slot, step in enumerate((1, 3, 2)):
        f1.append(
            send(quad.at[(zi + step) % 4], far.at[slot], (at((4, -4, 8)[slot], True), c))
        )
    for copy in f1:
        copy.wait_recv()
    mean = (quad[zi] + far[0] + far[1] + far[2]) * scale
    own[zi] = mean
    a1 = []
    for dz in (4, -4, 8):
        a1.append(send(own.at[zi], own.at[zi], (at(dz, True), c)))

    c3.wait_recv()
    for copy in w1:
        copy.wait_recv()
    backward = [wr[2 - a].reshape(256, 144).T for a in range(3)]
    for plane in range(2):
        conv(edge_weights(backward, plane), cg, plane)
        inp_ref[plane] = tap_sum(sums, -1, column).astype(jnp.bfloat16)

    for copy in a1:
        copy.wait_recv()
    full[pl.ds(mine * 4, 4)] = own[...]
    a2 = []
    for dz, same in moves:
        a2.append(send(own, full.at[pl.ds(mine * 4, 4)], (at(dz, same), c)))
    for copy in a2:
        copy.wait_recv()
    grad_ref[...] = full[0:27]
    for copy in begun:
        copy.wait_send()


def on_device(volume, kernel, cotangent):
    depth, chans, height, width = volume.shape
    cells = height * width
    nspace = lax.axis_size("space")
    scale = 1.0 / math.sqrt(depth * nspace * cells)
    vol = volume.reshape(depth, chans, cells)
    cot = cotangent.reshape(depth, chans, cells)
    kt = kernel.reshape(3, 9, 16, 16, 16).transpose(3, 0, 2, 1, 4).reshape(16, 3, 16, 144)
    vmem = pl.BlockSpec(memory_space=pltpu.VMEM)
    bf16, f32 = jnp.bfloat16, jnp.float32
    out, inp, grad = pl.pallas_call(
        functools.partial(layer_kernel, nspace, scale),
        out_shape=(
            jax.ShapeDtypeStruct((2, 16, 1024), bf16),
            jax.ShapeDtypeStruct((2, 16, 1024), bf16),
            jax.ShapeDtypeStruct((27, 16, 256), f32),
        ),
        in_specs=[vmem] * 4,
        out_specs=(vmem,) * 3,
        scratch_shapes=[
            pltpu.VMEM((4, 2, 4, 2, 16, 1024), bf16),
            pltpu.VMEM((4, 2, 4, 2, 16, 1024), bf16),
            pltpu.VMEM((3, 16, 16, 144), bf16),
            pltpu.VMEM((288, 1024), bf16),
            pltpu.VMEM((144, 1024), f32),
            pltpu.VMEM((32, 16, 256), f32),
            pltpu.VMEM((7, 4, 16, 256), f32),
            pltpu.VMEM((4, 16, 256), f32),
            pltpu.VMEM((3, 16, 256), f32),
            pltpu.VMEM((4, 16, 256), f32),
            pltpu.VMEM((32, 16, 256), f32),
            pltpu.SemaphoreType.DMA((COPIES,)),
            pltpu.SemaphoreType.DMA((COPIES,)),
        ],
        compiler_params=pltpu.CompilerParams(
            collective_id=0, has_side_effects=True, vmem_limit_bytes=48 << 20
        ),
        name="layer",
    )(vol, cot, kernel, kt)
    return (
        out.reshape(depth, chans, height, width),
        inp.reshape(depth, chans, height, width),
        grad,
    )


def solution(mesh):
    return jax.shard_map(
        on_device,
        mesh=mesh,
        in_specs=(
            P("space", "chan", None, None),
            P(None, "chan", None),
            P("space", "chan", None, None),
        ),
        out_specs=(
            P("space", "chan", None, None),
            P("space", "chan", None, None),
            P(None, "chan", None),
        ),
        check_vma=False,
    )
```

```python
import functools
import math

import jax
import jax.numpy as jnp
from jax import lax
from jax.experimental import pallas as pl
from jax.experimental.pallas import tpu as pltpu
from jax.sharding import PartitionSpec as P

MESH = pl.DeviceIdType.MESH
COPIES = 96


def col_shift(x, step, column):
    if step == 0:
        return x
    width = x.shape[1]
    if step == 1:
        moved = pltpu.roll(x, width - 1, 1)
        return jnp.where(column == 127, 0.0, moved)
    moved = pltpu.roll(x, 1, 1)
    return jnp.where(column == 0, 0.0, moved)


def row_shift(x, step):
    if step == 0:
        return x
    zeros = jnp.zeros((x.shape[0], 128), x.dtype)
    if step == 1:
        return jnp.concatenate([x[:, 128:], zeros], axis=1)
    return jnp.concatenate([zeros, x[:, :-128]], axis=1)


def tap_sum(sums_ref, sign, column):
    total = None
    for b in range(3):
        line = None
        for c in range(3):
            tap = 3 * b + c
            part = col_shift(sums_ref[16 * tap : 16 * tap + 16, :], sign * (c - 1), column)
            line = part if line is None else line + part
        moved = row_shift(line, sign * (b - 1))
        total = moved if total is None else total + moved
    return total


def layer_kernel(
    nspace,
    scale,
    vol_ref,
    cot_ref,
    ker_ref,
    out_ref,
    inp_ref,
    grad_ref,
    vg,
    cg,
    kt,
    wr,
    cs,
    sums,
    part,
    near,
    quad,
    far,
    own,
    full,
    send_sem,
    recv_sem,
    known_sem,
):
    s = lax.axis_index("space")
    c = lax.axis_index("chan")
    nz = nspace // 2
    z, x_lo = s // 2, s % 2
    x_hi, y, core = c // 8, (c // 2) % 4, c % 2
    flip = (1 - x_hi) * 8 + y * 2 + core
    mate = c + 1 - 2 * core

    def at(dz, same):
        zz = lax.rem(z + dz + nz, nz)
        xx = x_lo if same else 1 - x_lo
        return zz * 2 + xx

    pair = at(0, False)
    edge = lax.rem(s + nspace + 2 * x_lo - 1, nspace)

    def y_at(dy):
        return lax.rem(y + dy, 4)

    def chan_of(dy):
        return x_hi * 8 + y_at(dy) * 2 + core

    peers = [(s, mate), (s, flip)] + [(s, chan_of(dy)) for dy in (1, 2, 3)]
    peers += [(pair, c), (pair, flip), (edge, c), (edge, flip)]
    peers += [(at(1, True), c), (at(-1, True), c)]
    barrier = pltpu.get_barrier_semaphore()
    for peer in peers:
        pl.semaphore_signal(barrier, inc=1, device_id=peer, device_id_type=MESH)

    column = lax.broadcasted_iota(jnp.int32, (16, 1024), 1) % 128
    for plane in range(2):
        local = cot_ref[plane].astype(jnp.float32)
        for tap in range(9):
            b, cc = tap // 3, tap % 3
            moved = row_shift(col_shift(local, 1 - cc, column), 1 - b)
            cs[144 * plane + 16 * tap : 144 * plane + 16 * tap + 16, :] = moved.astype(jnp.bfloat16)
    vg[1:3, x_hi, y, core] = vol_ref[...]
    cg[1:3, x_hi, y, core] = cot_ref[...]
    taps = [ker_ref[t].astype(jnp.float32) for t in range(27)]
    filler = jnp.zeros((16, 80), jnp.float32)
    for to in range(16):
        lanes = slice(16 * to, 16 * to + 16)
        for a in range(3):
            row = jnp.concatenate([taps[9 * a + t][:, lanes] for t in range(8)], axis=1)
            kt[to, a] = row.astype(jnp.bfloat16)
        row = jnp.concatenate([taps[9 * a + 8][:, lanes] for a in range(3)] + [filler], axis=1)
        kt[to, 3] = row.astype(jnp.bfloat16)
    wr[:, c] = kt[c]
    pl.semaphore_wait(barrier, len(peers))

    def tell(stage, dz):
        for step in (dz, -dz):
            pl.semaphore_signal(
                known_sem.at[stage], inc=1, device_id=(at(step, True), c), device_id_type=MESH
            )

    tell(0, 1)

    count = [0]
    sent = []

    def copy_of(src, dst, peer, index=None):
        if index is None:
            index = count[0]
            count[0] += 1
        return pltpu.make_async_remote_copy(
            src_ref=src,
            dst_ref=dst,
            send_sem=send_sem.at[index],
            recv_sem=recv_sem.at[index],
            device_id=peer,
            device_id_type=MESH,
        )

    def send(src, dst, peer):
        copy = copy_of(src, dst, peer)
        copy.start()
        sent.append(copy)
        return copy

    def start(copies):
        for copy in copies:
            copy.start()

    def arrive(copies):
        for copy in copies:
            copy.wait_recv()

    def by_core(on_0, on_1):
        pl.when(core == 0)(on_0)
        pl.when(core == 1)(on_1)

    pair_src, pair_dst = 1 - x_lo, 3 * x_lo
    edge_src, edge_dst = x_lo, 3 * (1 - x_lo)
    middle = pl.ds(1, 2)

    def x_first(ref, g, lane):
        one = [copy_of(ref, g.at[middle, x_hi, y, lane], (s, flip))]
        for to in (c, flip):
            one.append(copy_of(ref.at[edge_src], g.at[edge_dst, x_hi, y, lane], (edge, to)))
        for to in (c, flip):
            one.append(copy_of(ref.at[pair_src], g.at[pair_dst, x_hi, y, lane], (pair, to)))
        block = g.at[:, :, y, lane]
        two = [copy_of(block, block, (s, chan_of(dy))) for dy in (1, 3, 2)]
        return one, two

    def y_first(ref, g, lane):
        one = [copy_of(ref, g.at[middle, x_hi, y, lane], (s, chan_of(dy))) for dy in (1, 3, 2)]
        block = g.at[middle, x_hi, :, lane]
        two = [copy_of(block, block, (s, flip))]
        for to in (c, flip):
            src = g.at[edge_src + 1, x_hi, :, lane]
            two.append(copy_of(src, g.at[edge_dst, x_hi, :, lane], (edge, to)))
        for to in (c, flip):
            src = g.at[pair_src + 1, x_hi, :, lane]
            two.append(copy_of(src, g.at[pair_dst, x_hi, :, lane], (pair, to)))
        return one, two

    def hand(blocks, lane_sems=None):
        return [
            copy_of(block, block, (s, mate), None if lane_sems is None else lane_sems[i])
            for i, block in enumerate(blocks)
        ]

    v0_one, v0_two = x_first(vol_ref, vg, 0)
    v1_one, v1_two = y_first(vol_ref, vg, 1)
    sems = list(range(count[0], count[0] + 4))
    count[0] += 4
    v0_hand = hand([vg.at[:, :, y_at(dy), 0] for dy in (0, 3, 1, 2)], sems)
    v1_hand = hand(
        [
            vg.at[middle, x_hi, :, 1],
            vg.at[middle, 1 - x_hi, :, 1],
            vg.at[3 * x_lo, :, :, 1],
            vg.at[3 * (1 - x_lo), :, :, 1],
        ],
        sems,
    )
    by_core(lambda: start(v0_one), lambda: start(v1_one))

    def v0_middle():
        arrive(v0_one)
        start(v0_two)
        v0_hand[0].start()

    def v1_middle():
        arrive(v1_one)
        start(v1_two)
        v1_hand[0].start()

    by_core(v0_middle, v1_middle)
    pl.semaphore_wait(known_sem.at[0], 2)
    tell(1, 2)

    def v0_late():
        for i in range(3):
            v0_two[i].wait_recv()
            v0_hand[i + 1].start()

    def v1_late():
        v1_two[0].wait_recv()
        v1_hand[1].start()
        arrive(v1_two[1:3])
        v1_hand[2].start()
        arrive(v1_two[3:5])
        v1_hand[3].start()

    by_core(v0_late, v1_late)

    c_one, c_two = x_first(cot_ref, cg, core)
    c_hand = hand([cg.at[:, :, y_at(dy), core] for dy in (0, 3, 1, 2)])
    start(c_one)
    pl.semaphore_wait(known_sem.at[1], 2)
    tell(2, 4)
    arrive(v0_hand)

    low = s == 0
    high = s == nspace - 1

    def plane_of(ref, index):
        return ref[index].reshape(256, 1024)

    def cell_dot(lhs, plane):
        return lax.dot_general(
            lhs, plane, (((1,), (1,)), ((), ())), preferred_element_type=jnp.float32
        )

    zero_rows = jnp.zeros((144, 256), jnp.float32)
    first = cell_dot(cs[0:144, :], plane_of(vg, 0))
    second = cell_dot(cs[...], plane_of(vg, 1))
    third = cell_dot(cs[...], plane_of(vg, 2))
    fourth = cell_dot(cs[144:288, :], plane_of(vg, 3))
    first = jnp.where(low, zero_rows, first)
    fourth = jnp.where(high, zero_rows, fourth)
    terms = [first + second[144:288], second[0:144] + third[144:288], third[0:144] + fourth]
    for a in range(3):
        term = terms[a].reshape(9, 2, 8, 256)
        for half in range(2):
            part[half, 9 * a : 9 * a + 9] = term[:, half]
    part[:, 27:32] = jnp.zeros((2, 5, 8, 256), jnp.float32)

    r = z % 4
    zi = z // 4
    mine = pl.ds((x_lo * 4 + r) * 4, 4)
    moves = [(1, True), (-1, True), (2, True), (1, False), (-1, False), (-2, False), (0, False)]
    n1 = []
    for half in range(2):
        n1.append([])
        for slot, (dz, same) in enumerate(moves):
            group = (x_lo if same else 1 - x_lo) * 4 + (r + dz + 4) % 4
            n1[half].append(
                send(part.at[half, pl.ds(group * 4, 4)], near.at[half, slot], (at(dz, same), c))
            )

    arrive(c_one)
    start(c_two)
    c_hand[0].start()

    def conv(weights, ref, first_plane):
        rows = ref[first_plane : first_plane + 3].reshape(768, 1024)
        sums[...] = jnp.dot(weights, rows, preferred_element_type=jnp.float32)

    blank = jnp.zeros((144, 256), jnp.bfloat16)

    def edge_weights(taps, plane):
        below, middle, above = taps
        if plane == 0:
            below = jnp.where(low, blank, below)
        else:
            above = jnp.where(high, blank, above)
        return jnp.concatenate([below, middle, above], axis=1)

    forward = [ker_ref[9 * a : 9 * a + 9].reshape(144, 256) for a in range(3)]
    for plane in range(2):
        conv(edge_weights(forward, plane), vg, plane)
        out_ref[plane] = tap_sum(sums, 1, column).astype(jnp.bfloat16)

    pl.semaphore_wait(known_sem.at[2], 2)
    f1 = []
    for half in range(2):
        arrive(n1[half])
        total = part[half, mine]
        for slot in range(7):
            total = total + near[half, slot]
        quad[half] = total
        f1.append(
            [
                send(quad.at[half, (zi + step) % 4], far.at[half, slot], (at(dz, True), c))
                for slot, (step, dz) in enumerate(((1, 4), (3, -4), (2, 8)))
            ]
        )

    w1 = []
    for m in range(1, 16):
        to = lax.rem(c + m, 16)
        w1.append(send(kt.at[to], wr.at[:, c], (s, to)))

    a1 = []
    for half in range(2):
        arrive(f1[half])
        total = quad[half, zi] + far[half, 0] + far[half, 1] + far[half, 2]
        own[half, zi] = total * scale
        a1.append(
            [send(own.at[half, zi], own.at[half, zi], (at(dz, True), c)) for dz in (4, -4, 8)]
        )

    for i in range(3):
        c_two[i].wait_recv()
        c_hand[i + 1].start()

    a2 = []
    for half in range(2):
        arrive(a1[half])
        full[half, mine] = own[half]
        for dz, same in moves:
            a2.append(send(own.at[half], full.at[half, mine], (at(dz, same), c)))

    arrive(c_hand)
    arrive(w1)
    last = wr[3].reshape(256, 128)
    backward = []
    for a in (2, 1, 0):
        lines = jnp.concatenate(
            [wr[a].reshape(256, 128), last[:, 16 * a : 16 * a + 16]], axis=1
        )
        backward.append(lines.T)
    for plane in range(2):
        conv(edge_weights(backward, plane), cg, plane)
        inp_ref[plane] = tap_sum(sums, -1, column).astype(jnp.bfloat16)

    arrive(a2)
    for half in range(2):
        grad_ref[:, 8 * half : 8 * half + 8] = full[half, 0:27]

    def ended(copies):
        for copy in copies:
            copy.wait_send()

    by_core(
        lambda: ended(v0_one + v0_two + v0_hand),
        lambda: ended(v1_one + v1_two + v1_hand),
    )
    ended(c_one + c_two + c_hand + sent)


def on_device(volume, kernel, cotangent):
    depth, chans, height, width = volume.shape
    cells = height * width
    nspace = lax.axis_size("space")
    scale = 1.0 / math.sqrt(depth * nspace * cells)
    vol = volume.reshape(depth, chans, cells)
    cot = cotangent.reshape(depth, chans, cells)
    vmem = pl.BlockSpec(memory_space=pltpu.VMEM)
    bf16, f32 = jnp.bfloat16, jnp.float32
    out, inp, grad = pl.pallas_call(
        functools.partial(layer_kernel, nspace, scale),
        out_shape=(
            jax.ShapeDtypeStruct((2, 16, 1024), bf16),
            jax.ShapeDtypeStruct((2, 16, 1024), bf16),
            jax.ShapeDtypeStruct((27, 16, 256), f32),
        ),
        in_specs=[vmem] * 3,
        out_specs=(vmem,) * 3,
        scratch_shapes=[
            pltpu.VMEM((4, 2, 4, 2, 16, 1024), bf16),
            pltpu.VMEM((4, 2, 4, 2, 16, 1024), bf16),
            pltpu.VMEM((16, 4, 16, 128), bf16),
            pltpu.VMEM((4, 16, 16, 128), bf16),
            pltpu.VMEM((288, 1024), bf16),
            pltpu.VMEM((144, 1024), f32),
            pltpu.VMEM((2, 32, 8, 256), f32),
            pltpu.VMEM((2, 7, 4, 8, 256), f32),
            pltpu.VMEM((2, 4, 8, 256), f32),
            pltpu.VMEM((2, 3, 8, 256), f32),
            pltpu.VMEM((2, 4, 8, 256), f32),
            pltpu.VMEM((2, 32, 8, 256), f32),
            pltpu.SemaphoreType.DMA((COPIES,)),
            pltpu.SemaphoreType.DMA((COPIES,)),
            pltpu.SemaphoreType.REGULAR((3,)),
        ],
        compiler_params=pltpu.CompilerParams(
            collective_id=0, has_side_effects=True, vmem_limit_bytes=48 << 20
        ),
        name="layer",
    )(vol, cot, kernel)
    return (
        out.reshape(depth, chans, height, width),
        inp.reshape(depth, chans, height, width),
        grad,
    )


def solution(mesh):
    return jax.shard_map(
        on_device,
        mesh=mesh,
        in_specs=(
            P("space", "chan", None, None),
            P(None, "chan", None),
            P("space", "chan", None, None),
        ),
        out_specs=(
            P("space", "chan", None, None),
            P("space", "chan", None, None),
            P(None, "chan", None),
        ),
        check_vma=False,
    )
```

```python
import functools
import math

import jax
import jax.numpy as jnp
from jax import lax
from jax.experimental import pallas as pl
from jax.experimental.pallas import tpu as pltpu
from jax.sharding import PartitionSpec as P

MESH = pl.DeviceIdType.MESH
COPIES = 112


def col_shift(x, step, column):
    if step == 0:
        return x
    width = x.shape[1]
    if step == 1:
        moved = pltpu.roll(x, width - 1, 1)
        return jnp.where(column == 127, 0.0, moved)
    moved = pltpu.roll(x, 1, 1)
    return jnp.where(column == 0, 0.0, moved)


def row_shift(x, step):
    if step == 0:
        return x
    zeros = jnp.zeros((x.shape[0], 128), x.dtype)
    if step == 1:
        return jnp.concatenate([x[:, 128:], zeros], axis=1)
    return jnp.concatenate([zeros, x[:, :-128]], axis=1)


def tap_sum(sums_ref, sign, column):
    total = None
    for b in range(3):
        line = None
        for c in range(3):
            tap = 3 * b + c
            part = col_shift(sums_ref[16 * tap : 16 * tap + 16, :], sign * (c - 1), column)
            line = part if line is None else line + part
        moved = row_shift(line, sign * (b - 1))
        total = moved if total is None else total + moved
    return total


def layer_kernel(
    nspace,
    scale,
    vol_ref,
    cot_ref,
    ker_ref,
    out_ref,
    inp_ref,
    grad_ref,
    vol,
    cot,
    rim,
    vg,
    cg,
    kt,
    wr,
    cs,
    sums,
    part,
    near,
    quad,
    far,
    own,
    full,
    send_sem,
    recv_sem,
    known_sem,
):
    s = lax.axis_index("space")
    c = lax.axis_index("chan")
    nz = nspace // 2
    z, x_lo = s // 2, s % 2
    x_hi, y, core = c // 8, (c // 2) % 4, c % 2
    flip = (1 - x_hi) * 8 + y * 2 + core
    mate = c + 1 - 2 * core

    def at(dz, same):
        zz = lax.rem(z + dz + nz, nz)
        xx = x_lo if same else 1 - x_lo
        return zz * 2 + xx

    pair = at(0, False)
    edge = lax.rem(s + nspace + 2 * x_lo - 1, nspace)

    def y_at(dy):
        return lax.rem(y + dy, 4)

    def chan_of(dy):
        return x_hi * 8 + y_at(dy) * 2 + core

    peers = [(s, mate), (s, flip)] + [(s, chan_of(dy)) for dy in (1, 2, 3)]
    peers += [(pair, c), (pair, flip), (edge, c), (edge, flip)]
    peers += [(at(1, True), c), (at(-1, True), c)]
    barrier = pltpu.get_barrier_semaphore()
    for peer in peers:
        pl.semaphore_signal(barrier, inc=1, device_id=peer, device_id_type=MESH)

    for plane in range(2):
        block = vol_ref[plane].astype(jnp.float32).reshape(16, 1024)
        vol[plane] = block.astype(jnp.bfloat16)
        vg[plane, x_hi, y, core] = block.astype(jnp.bfloat16)
        block = cot_ref[plane].astype(jnp.float32).reshape(16, 1024)
        cot[plane] = block.astype(jnp.bfloat16)
        cg[plane, x_hi, y, core] = block.astype(jnp.bfloat16)
    pl.semaphore_wait(barrier, len(peers))

    count = [0]
    sent = []

    def copy_of(src, dst, peer, index=None):
        if index is None:
            index = count[0]
            count[0] += 1
        return pltpu.make_async_remote_copy(
            src_ref=src,
            dst_ref=dst,
            send_sem=send_sem.at[index],
            recv_sem=recv_sem.at[index],
            device_id=peer,
            device_id_type=MESH,
        )

    def send(src, dst, peer):
        copy = copy_of(src, dst, peer)
        copy.start()
        sent.append(copy)
        return copy

    def start(copies):
        for copy in copies:
            copy.start()

    def arrive(copies):
        for copy in copies:
            copy.wait_recv()

    def ended(copies):
        for copy in copies:
            copy.wait_send()

    def by_core(on_0, on_1):
        pl.when(core == 0)(on_0)
        pl.when(core == 1)(on_1)

    def tell(stage, dz):
        for step in (dz, -dz):
            pl.semaphore_signal(
                known_sem.at[stage], inc=1, device_id=(at(step, True), c), device_id_type=MESH
            )

    pair_src, pair_dst = 1 - x_lo, 2 + x_lo
    edge_src, edge_dst = x_lo, 3 - x_lo
    mine, rims = pl.ds(0, 2), pl.ds(2, 2)

    def hand(blocks, shared=None):
        return [
            copy_of(block, block, (s, mate), None if shared is None else shared[i])
            for i, block in enumerate(blocks)
        ]

    def to_y(src, dst):
        return [copy_of(src, dst, (s, chan_of(dy))) for dy in (1, 3, 2)]

    def to_rims(sources, targets):
        copies = [copy_of(sources[0], targets[0], (edge, to)) for to in (c, flip)]
        return copies + [copy_of(sources[1], targets[1], (pair, to)) for to in (c, flip)]

    def own_rims(block, g, lane):
        return to_rims(
            (block.at[edge_src], block.at[pair_src]),
            (g.at[edge_dst, x_hi, y, lane], g.at[pair_dst, x_hi, y, lane]),
        )

    def shared_sems():
        count[0] += 4
        return list(range(count[0] - 4, count[0]))

    v0_one = [copy_of(vol, vg.at[mine, x_hi, y, 0], (s, flip))]
    v0_two = to_y(vg.at[mine, :, y, 0], vg.at[mine, :, y, 0])
    v1_one = to_y(vol, vg.at[mine, x_hi, y, 1])
    v1_two = [
        copy_of(vg.at[p, x_hi, :, 1], vg.at[p, x_hi, :, 1], (s, flip)) for p in range(2)
    ]
    sems = shared_sems()
    v0_hand = hand([vg.at[mine, :, y_at(dy), 0] for dy in (0, 3, 1, 2)], sems)
    v1_hand = hand(
        [vg.at[p, side, :, 1] for side in (x_hi, 1 - x_hi) for p in range(2)], sems
    )
    by_core(lambda: start(v0_one), lambda: start(v1_one))
    beside = [
        send(cot.at[edge_src], rim.at[edge_dst - 2], (edge, c)),
        send(cot.at[pair_src], rim.at[pair_dst - 2], (pair, c)),
    ]
    tell(0, 1)

    column = lax.broadcasted_iota(jnp.int32, (16, 1024), 1) % 128
    low = s == 0
    high = s == nspace - 1

    def spread(block, slot):
        for tap in range(9):
            b, cc = tap // 3, tap % 3
            moved = row_shift(col_shift(block, 1 - cc, column), 1 - b)
            first = 144 * slot + 16 * tap
            cs[first : first + 16, :] = moved.astype(jnp.bfloat16)

    for plane in range(2):
        spread(cot[plane].astype(jnp.float32), plane + 1)

    def v0_middle():
        arrive(v0_one)
        start(v0_two)
        v0_hand[0].start()

    def v1_middle():
        arrive(v1_one)
        start(v1_two)
        start(v1_hand[0:2])

    by_core(v0_middle, v1_middle)

    taps = [ker_ref[t].astype(jnp.float32) for t in range(27)]
    filler = jnp.zeros((16, 80), jnp.float32)
    for to in range(16):
        lanes = slice(16 * to, 16 * to + 16)
        for a in range(3):
            row = jnp.concatenate([taps[9 * a + t][:, lanes] for t in range(8)], axis=1)
            kt[to, a] = row.astype(jnp.bfloat16)
        row = jnp.concatenate([taps[9 * a + 8][:, lanes] for a in range(3)] + [filler], axis=1)
        kt[to, 3] = row.astype(jnp.bfloat16)
    wr[:, c] = kt[c]

    pl.semaphore_wait(known_sem.at[0], 2)
    tell(1, 2)
    arrive(beside)
    below = rim[0].astype(jnp.float32)
    above = rim[1].astype(jnp.float32)
    spread(jnp.where(low, jnp.zeros_like(below), below), 0)
    spread(jnp.where(high, jnp.zeros_like(above), above), 3)

    def v0_late():
        for i in range(3):
            v0_two[i].wait_recv()
            v0_hand[i + 1].start()

    def v1_late():
        for i in range(2):
            v1_two[i].wait_recv()
            v1_hand[i + 2].start()

    by_core(v0_late, v1_late)

    r_one = own_rims(vol, vg, core)
    r_two = to_y(vg.at[rims, :, y, core], vg.at[rims, :, y, core])
    r_hand = hand([vg.at[rims, :, y_at(dy), core] for dy in (0, 3, 1, 2)])
    start(r_one)
    c0_one = [copy_of(cot, cg.at[mine, x_hi, y, 0], (s, flip))] + own_rims(cot, cg, 0)
    c0_two = to_y(cg.at[:, :, y, 0], cg.at[:, :, y, 0])
    c1_one = to_y(cot, cg.at[mine, x_hi, y, 1])
    c1_two = [copy_of(cg.at[mine, x_hi, :, 1], cg.at[mine, x_hi, :, 1], (s, flip))]
    c1_two += to_rims(
        (cg.at[edge_src, x_hi, :, 1], cg.at[pair_src, x_hi, :, 1]),
        (cg.at[edge_dst, x_hi, :, 1], cg.at[pair_dst, x_hi, :, 1]),
    )
    sems = shared_sems()
    c0_hand = hand([cg.at[:, :, y_at(dy), 0] for dy in (0, 3, 1, 2)], sems)
    c1_hand = hand(
        [
            cg.at[mine, x_hi, :, 1],
            cg.at[mine, 1 - x_hi, :, 1],
            cg.at[2 + x_lo, :, :, 1],
            cg.at[3 - x_lo, :, :, 1],
        ],
        sems,
    )
    by_core(lambda: start(c0_one), lambda: start(c1_one))

    pl.semaphore_wait(known_sem.at[1], 2)
    tell(2, 4)
    arrive(v0_hand)

    def cell_dot(lhs, plane):
        return lax.dot_general(
            lhs,
            vg[plane].reshape(256, 1024),
            (((1,), (1,)), ((), ())),
            preferred_element_type=jnp.float32,
        )

    term = cell_dot(cs[0:432, :], 0) + cell_dot(cs[144:576, :], 1)
    for half in range(2):
        for a in range(3):
            rows = term[144 * (2 - a) : 144 * (3 - a), 128 * half : 128 * half + 128]
            part[half, 18 * a : 18 * a + 18] = rows.reshape(18, 8, 128)
    part[:, 54:56] = jnp.zeros((2, 2, 8, 128), jnp.float32)
    quad[:, 7] = jnp.zeros((2, 8, 128), jnp.float32)

    r = z % 4
    zi = z // 4
    held = pl.ds((x_lo * 4 + r) * 7, 7)
    moves = [(2, True), (-2, False), (1, True), (-1, True), (1, False), (-1, False), (0, False)]
    n1 = []
    for half in range(2):
        n1.append([])
        for slot, (dz, same) in enumerate(moves):
            group = (x_lo if same else 1 - x_lo) * 4 + (r + dz + 4) % 4
            n1[half].append(
                send(part.at[half, pl.ds(group * 7, 7)], near.at[half, slot], (at(dz, same), c))
            )

    arrive(r_one)
    start(r_two)
    r_hand[0].start()

    pl.semaphore_wait(known_sem.at[2], 2)
    f1 = []
    for half in range(2):
        arrive(n1[half])
        total = part[half, held]
        for slot in range(7):
            total = total + near[half, slot]
        quad[half, 0:7] = total
        f1.append([])
        for slot, (step, dz) in enumerate(((2, 8), (1, 4), (3, -4))):
            tiles = pl.ds(2 * ((zi + step) % 4), 2)
            f1[half].append(send(quad.at[half, tiles], far.at[half, slot], (at(dz, True), c)))

    def c0_middle():
        arrive(c0_one)
        start(c0_two)
        c0_hand[0].start()

    def c1_middle():
        arrive(c1_one)
        start(c1_two)
        c1_hand[0].start()

    by_core(c0_middle, c1_middle)
    w1 = []
    for m in range(1, 16):
        to = lax.rem(c + m, 16)
        w1.append(send(kt.at[to], wr.at[:, c], (s, to)))

    def conv(weights, g, plane):
        order = (2, 0, 1) if plane == 0 else (0, 1, 3)
        total = None
        for taps_of, index in zip(weights, order):
            if index == 2:
                taps_of = jnp.where(low, jnp.zeros_like(taps_of), taps_of)
            if index == 3:
                taps_of = jnp.where(high, jnp.zeros_like(taps_of), taps_of)
            rows = g[index].reshape(256, 1024)
            product = jnp.dot(taps_of, rows, preferred_element_type=jnp.float32)
            total = product if total is None else total + product
        sums[...] = total

    for i in range(3):
        r_two[i].wait_recv()
        r_hand[i + 1].start()
    arrive(r_hand)
    forward = [ker_ref[9 * a : 9 * a + 9].reshape(144, 256) for a in range(3)]
    for plane in range(2):
        conv(forward, vg, plane)
        out_ref[plane] = tap_sum(sums, 1, column).reshape(16, 8, 128).astype(jnp.bfloat16)

    a1 = []
    chunk = pl.ds(2 * zi, 2)
    for half in range(2):
        arrive(f1[half])
        total = quad[half, chunk] + far[half, 0] + far[half, 1] + far[half, 2]
        own[half, chunk] = total * scale
        a1.append(
            [send(own.at[half, chunk], own.at[half, chunk], (at(dz, True), c)) for dz in (8, 4, -4)]
        )

    def c0_late():
        for i in range(3):
            c0_two[i].wait_recv()
            c0_hand[i + 1].start()

    def c1_late():
        c1_two[0].wait_recv()
        c1_hand[1].start()
        arrive(c1_two[1:3])
        c1_hand[2].start()
        arrive(c1_two[3:5])
        c1_hand[3].start()

    by_core(c0_late, c1_late)

    a2 = []
    for half in range(2):
        arrive(a1[half])
        full[half, held] = own[half, 0:7]
        for dz, same in moves:
            a2.append(send(own.at[half, pl.ds(0, 7)], full.at[half, held], (at(dz, same), c)))

    arrive(c0_hand)
    arrive(w1)
    last = wr[3].reshape(256, 128)
    backward = []
    for a in (2, 1, 0):
        lines = jnp.concatenate(
            [wr[a].reshape(256, 128), last[:, 16 * a : 16 * a + 16]], axis=1
        )
        backward.append(lines.T)
    for plane in range(2):
        conv(backward, cg, plane)
        inp_ref[plane] = tap_sum(sums, -1, column).reshape(16, 8, 128).astype(jnp.bfloat16)

    arrive(a2)
    for half in range(2):
        grad_ref[:, :, 128 * half : 128 * half + 128] = full[half, 0:54].reshape(27, 16, 128)

    by_core(
        lambda: ended(v0_one + v0_two + v0_hand + c0_one + c0_two + c0_hand),
        lambda: ended(v1_one + v1_two + v1_hand + c1_one + c1_two + c1_hand),
    )
    ended(r_one + r_two + r_hand + sent)


def on_device(volume, kernel, cotangent):
    depth, chans, height, width = volume.shape
    nspace = lax.axis_size("space")
    scale = 1.0 / math.sqrt(depth * nspace * height * width)
    vmem = pl.BlockSpec(memory_space=pltpu.VMEM)
    bf16, f32 = jnp.bfloat16, jnp.float32
    return pl.pallas_call(
        functools.partial(layer_kernel, nspace, scale),
        out_shape=(
            jax.ShapeDtypeStruct(volume.shape, bf16),
            jax.ShapeDtypeStruct(volume.shape, bf16),
            jax.ShapeDtypeStruct((27, 16, 256), f32),
        ),
        in_specs=[vmem] * 3,
        out_specs=(vmem,) * 3,
        scratch_shapes=[
            pltpu.VMEM((2, 16, 1024), bf16),
            pltpu.VMEM((2, 16, 1024), bf16),
            pltpu.VMEM((2, 16, 1024), bf16),
            pltpu.VMEM((4, 2, 4, 2, 16, 1024), bf16),
            pltpu.VMEM((4, 2, 4, 2, 16, 1024), bf16),
            pltpu.VMEM((16, 4, 16, 128), bf16),
            pltpu.VMEM((4, 16, 16, 128), bf16),
            pltpu.VMEM((576, 1024), bf16),
            pltpu.VMEM((144, 1024), f32),
            pltpu.VMEM((2, 56, 8, 128), f32),
            pltpu.VMEM((2, 7, 7, 8, 128), f32),
            pltpu.VMEM((2, 8, 8, 128), f32),
            pltpu.VMEM((2, 3, 2, 8, 128), f32),
            pltpu.VMEM((2, 8, 8, 128), f32),
            pltpu.VMEM((2, 56, 8, 128), f32),
            pltpu.SemaphoreType.DMA((COPIES,)),
            pltpu.SemaphoreType.DMA((COPIES,)),
            pltpu.SemaphoreType.REGULAR((3,)),
        ],
        compiler_params=pltpu.CompilerParams(
            collective_id=0, has_side_effects=True, vmem_limit_bytes=48 << 20
        ),
        name="layer",
    )(volume, cotangent, kernel)


def solution(mesh):
    return jax.shard_map(
        on_device,
        mesh=mesh,
        in_specs=(
            P("space", "chan", None, None),
            P(None, "chan", None),
            P("space", "chan", None, None),
        ),
        out_specs=(
            P("space", "chan", None, None),
            P("space", "chan", None, None),
            P(None, "chan", None),
        ),
        check_vma=False,
    )
```

```python
import functools
import math

import jax
import jax.numpy as jnp
from jax import lax
from jax.experimental import pallas as pl
from jax.experimental.pallas import tpu as pltpu
from jax.sharding import PartitionSpec as P

MESH = pl.DeviceIdType.MESH
COPIES = 112


def col_shift(x, step, column):
    if step == 0:
        return x
    width = x.shape[1]
    if step == 1:
        moved = pltpu.roll(x, width - 1, 1)
        return jnp.where(column == 127, 0.0, moved)
    moved = pltpu.roll(x, 1, 1)
    return jnp.where(column == 0, 0.0, moved)


def row_shift(x, step):
    if step == 0:
        return x
    zeros = jnp.zeros((x.shape[0], 128), x.dtype)
    if step == 1:
        return jnp.concatenate([x[:, 128:], zeros], axis=1)
    return jnp.concatenate([zeros, x[:, :-128]], axis=1)


def tap_sum(sums_ref, sign, column):
    total = None
    for b in range(3):
        line = None
        for c in range(3):
            tap = 3 * b + c
            part = col_shift(sums_ref[16 * tap : 16 * tap + 16, :], sign * (c - 1), column)
            line = part if line is None else line + part
        moved = row_shift(line, sign * (b - 1))
        total = moved if total is None else total + moved
    return total


def layer_kernel(
    nspace,
    scale,
    vol_ref,
    cot_ref,
    ker_ref,
    out_ref,
    inp_ref,
    grad_ref,
    vol,
    cot,
    rim,
    vg,
    cg,
    kt,
    wr,
    cs,
    sums,
    part,
    near,
    quad,
    far,
    own,
    full,
    send_sem,
    recv_sem,
    known_sem,
):
    s = lax.axis_index("space")
    c = lax.axis_index("chan")
    nz = nspace // 2
    z, x_lo = s // 2, s % 2
    x_hi, y, core = c // 8, (c // 2) % 4, c % 2
    flip = (1 - x_hi) * 8 + y * 2 + core
    mate = c + 1 - 2 * core

    def at(dz, same):
        zz = lax.rem(z + dz + nz, nz)
        xx = x_lo if same else 1 - x_lo
        return zz * 2 + xx

    pair = at(0, False)
    edge = lax.rem(s + nspace + 2 * x_lo - 1, nspace)

    def y_at(dy):
        return lax.rem(y + dy, 4)

    def chan_of(dy):
        return x_hi * 8 + y_at(dy) * 2 + core

    peers = [(s, mate), (s, flip)] + [(s, chan_of(dy)) for dy in (1, 2, 3)]
    peers += [(pair, c), (pair, flip), (edge, c), (edge, flip)]
    peers += [(at(1, True), c), (at(-1, True), c)]
    barrier = pltpu.get_barrier_semaphore()
    for peer in peers:
        pl.semaphore_signal(barrier, inc=1, device_id=peer, device_id_type=MESH)

    for plane in range(2):
        block = vol_ref[plane].astype(jnp.float32).reshape(16, 1024)
        vol[plane] = block.astype(jnp.bfloat16)
        vg[plane, x_hi, y, core] = block.astype(jnp.bfloat16)
        block = cot_ref[plane].astype(jnp.float32).reshape(16, 1024)
        cot[plane] = block.astype(jnp.bfloat16)
        cg[plane, x_hi, y, core] = block.astype(jnp.bfloat16)
    pl.semaphore_wait(barrier, len(peers))

    count = [0]
    sent = []

    def copy_of(src, dst, peer, index=None):
        if index is None:
            index = count[0]
            count[0] += 1
        return pltpu.make_async_remote_copy(
            src_ref=src,
            dst_ref=dst,
            send_sem=send_sem.at[index],
            recv_sem=recv_sem.at[index],
            device_id=peer,
            device_id_type=MESH,
        )

    def send(src, dst, peer):
        copy = copy_of(src, dst, peer)
        copy.start()
        sent.append(copy)
        return copy

    def start(copies):
        for copy in copies:
            copy.start()

    def arrive(copies):
        for copy in copies:
            copy.wait_recv()

    def ended(copies):
        for copy in copies:
            copy.wait_send()

    def by_core(on_0, on_1):
        pl.when(core == 0)(on_0)
        pl.when(core == 1)(on_1)

    def tell(stage, dz):
        for step in (dz, -dz):
            pl.semaphore_signal(
                known_sem.at[stage], inc=1, device_id=(at(step, True), c), device_id_type=MESH
            )

    pair_src, pair_dst = 1 - x_lo, 2 + x_lo
    edge_src, edge_dst = x_lo, 3 - x_lo
    mine, rims = pl.ds(0, 2), pl.ds(2, 2)

    def hand(blocks, shared=None):
        return [
            copy_of(block, block, (s, mate), None if shared is None else shared[i])
            for i, block in enumerate(blocks)
        ]

    def to_y(src, dst):
        return [copy_of(src, dst, (s, chan_of(dy))) for dy in (1, 3, 2)]

    def to_rims(sources, targets):
        copies = [copy_of(sources[0], targets[0], (edge, to)) for to in (c, flip)]
        return copies + [copy_of(sources[1], targets[1], (pair, to)) for to in (c, flip)]

    def own_rims(block, g, lane):
        return to_rims(
            (block.at[edge_src], block.at[pair_src]),
            (g.at[edge_dst, x_hi, y, lane], g.at[pair_dst, x_hi, y, lane]),
        )

    def shared_sems():
        count[0] += 4
        return list(range(count[0] - 4, count[0]))

    own_block = vg.at[mine, x_hi, y, core]
    v_y = to_y(vol, own_block)
    v_x = copy_of(vol, own_block, (s, flip))
    start(v_y[0:2])
    v_x.start()
    v_y[2].start()
    sides = (x_hi, 1 - x_hi)
    steps = (0, 3, 1, 2)
    hand_one = hand([vg.at[mine, sides[0], y_at(dy), core] for dy in steps])
    hand_two = hand([vg.at[mine, sides[1], y_at(dy), core] for dy in steps])
    sems = shared_sems()
    v0_two = [
        copy_of(
            vg.at[mine, sides[1], y, 0], vg.at[mine, sides[1], y, 0], (s, chan_of(dy)), sems[i]
        )
        for i, dy in enumerate((1, 3, 2))
    ]
    v1_two = [
        copy_of(
            vg.at[mine, sides[0], y_at(dy), 1],
            vg.at[mine, sides[0], y_at(dy), 1],
            (s, flip),
            sems[i],
        )
        for i, dy in enumerate((3, 1, 2))
    ]
    beside = [
        send(cot.at[edge_src], rim.at[edge_dst - 2], (edge, c)),
        send(cot.at[pair_src], rim.at[pair_dst - 2], (pair, c)),
    ]
    tell(0, 1)

    column = lax.broadcasted_iota(jnp.int32, (16, 1024), 1) % 128
    low = s == 0
    high = s == nspace - 1

    def spread(block, slot):
        for tap in range(9):
            b, cc = tap // 3, tap % 3
            moved = row_shift(col_shift(block, 1 - cc, column), 1 - b)
            first = 144 * slot + 16 * tap
            cs[first : first + 16, :] = moved.astype(jnp.bfloat16)

    for plane in range(2):
        spread(cot[plane].astype(jnp.float32), plane + 1)

    hand_one[0].start()
    v_x.wait_recv()
    pl.when(core == 0)(lambda: start(v0_two))
    hand_two[0].start()
    for i in range(3):
        v_y[i].wait_recv()
        pl.when(core == 1)(v1_two[i].start)
        hand_one[i + 1].start()
    pl.semaphore_wait(known_sem.at[0], 2)
    tell(1, 2)
    arrive(beside)
    below = rim[0].astype(jnp.float32)
    above = rim[1].astype(jnp.float32)
    spread(jnp.where(low, jnp.zeros_like(below), below), 0)
    spread(jnp.where(high, jnp.zeros_like(above), above), 3)

    pl.semaphore_wait(known_sem.at[1], 2)
    arrive(hand_one)

    def cell_dot(lhs, plane, half):
        return lax.dot_general(
            lhs,
            vg[plane, sides[half]].reshape(128, 1024),
            (((1,), (1,)), ((), ())),
            preferred_element_type=jnp.float32,
        )

    r = z % 4
    zi = z // 4
    held = pl.ds((x_lo * 4 + r) * 7, 7)
    moves = [(2, True), (-2, False), (1, True), (-1, True), (1, False), (-1, False), (0, False)]
    n1 = []

    def reduce_near(half):
        term = cell_dot(cs[0:432, :], 0, half) + cell_dot(cs[144:576, :], 1, half)
        for a in range(3):
            rows = term[144 * (2 - a) : 144 * (3 - a)]
            part[half, 18 * a : 18 * a + 18] = rows.reshape(18, 8, 128)
        part[half, 54:56] = jnp.zeros((2, 8, 128), jnp.float32)
        n1.append([])
        for slot, (dz, same) in enumerate(moves):
            group = (x_lo if same else 1 - x_lo) * 4 + (r + dz + 4) % 4
            n1[half].append(
                send(part.at[half, pl.ds(group * 7, 7)], near.at[half, slot], (at(dz, same), c))
            )

    reduce_near(0)

    for i in range(3):
        pl.when(core == 0)(v0_two[i].wait_recv)
        pl.when(core == 1)(v1_two[i].wait_recv)
        hand_two[i + 1].start()

    r_one = own_rims(vol, vg, core)
    r_two = to_y(vg.at[rims, :, y, core], vg.at[rims, :, y, core])
    r_hand = hand([vg.at[rims, :, y_at(dy), core] for dy in (0, 3, 1, 2)])
    start(r_one)
    c0_one = [copy_of(cot, cg.at[mine, x_hi, y, 0], (s, flip))] + own_rims(cot, cg, 0)
    c0_two = to_y(cg.at[:, :, y, 0], cg.at[:, :, y, 0])
    c1_one = to_y(cot, cg.at[mine, x_hi, y, 1])
    c1_two = [copy_of(cg.at[mine, x_hi, :, 1], cg.at[mine, x_hi, :, 1], (s, flip))]
    c1_two += to_rims(
        (cg.at[edge_src, x_hi, :, 1], cg.at[pair_src, x_hi, :, 1]),
        (cg.at[edge_dst, x_hi, :, 1], cg.at[pair_dst, x_hi, :, 1]),
    )
    sems = shared_sems()
    c0_hand = hand([cg.at[:, :, y_at(dy), 0] for dy in (0, 3, 1, 2)], sems)
    c1_hand = hand(
        [
            cg.at[mine, x_hi, :, 1],
            cg.at[mine, 1 - x_hi, :, 1],
            cg.at[2 + x_lo, :, :, 1],
            cg.at[3 - x_lo, :, :, 1],
        ],
        sems,
    )
    by_core(lambda: start(c0_one), lambda: start(c1_one))

    arrive(hand_two)
    reduce_near(1)

    arrive(r_one)
    start(r_two)
    r_hand[0].start()

    hop = [at(4 * (1 - 2 * ((zi + r + i) % 2)), True) for i in range(2)]

    def exchange(half, step):
        return send(quad.at[half, step], far.at[half, step], (hop[(half + step) % 2], c))

    f1 = []
    for half in range(2):
        arrive(n1[half])
        total = part[half, held]
        for slot in range(7):
            total = total + near[half, slot]
        quad[half, 0] = total
        f1.append(exchange(half, 0))

    def c0_middle():
        arrive(c0_one)
        start(c0_two)
        c0_hand[0].start()

    def c1_middle():
        arrive(c1_one)
        start(c1_two)
        c1_hand[0].start()

    by_core(c0_middle, c1_middle)
    taps = [ker_ref[t].astype(jnp.float32) for t in range(27)]
    filler = jnp.zeros((16, 80), jnp.float32)
    for to in range(16):
        lanes = slice(16 * to, 16 * to + 16)
        for a in range(3):
            row = jnp.concatenate([taps[9 * a + t][:, lanes] for t in range(8)], axis=1)
            kt[to, a] = row.astype(jnp.bfloat16)
        row = jnp.concatenate([taps[9 * a + 8][:, lanes] for a in range(3)] + [filler], axis=1)
        kt[to, 3] = row.astype(jnp.bfloat16)
    wr[:, c] = kt[c]

    w1 = []
    for m in range(1, 16):
        to = lax.rem(c + m, 16)
        w1.append(send(kt.at[to], wr.at[:, c], (s, to)))

    def conv(weights, g, plane):
        order = (2, 0, 1) if plane == 0 else (0, 1, 3)
        total = None
        for taps_of, index in zip(weights, order):
            if index == 2:
                taps_of = jnp.where(low, jnp.zeros_like(taps_of), taps_of)
            if index == 3:
                taps_of = jnp.where(high, jnp.zeros_like(taps_of), taps_of)
            rows = g[index].reshape(256, 1024)
            product = jnp.dot(taps_of, rows, preferred_element_type=jnp.float32)
            total = product if total is None else total + product
        sums[...] = total

    f2 = []
    for half in range(2):
        f1[half].wait_recv()
        quad[half, 1] = quad[half, 0] + far[half, 0]
        f2.append(exchange(half, 1))

    for i in range(3):
        r_two[i].wait_recv()
        r_hand[i + 1].start()
    arrive(r_hand)
    forward = [ker_ref[9 * a : 9 * a + 9].reshape(144, 256) for a in range(3)]
    for plane in range(2):
        conv(forward, vg, plane)
        out_ref[plane] = tap_sum(sums, 1, column).reshape(16, 8, 128).astype(jnp.bfloat16)

    a2 = []
    for half in range(2):
        f2[half].wait_recv()
        total = (quad[half, 1] + far[half, 1]) * scale
        own[half] = total
        full[half, held] = total
        for dz, same in moves:
            a2.append(send(own.at[half], full.at[half, held], (at(dz, same), c)))

    def c0_late():
        for i in range(3):
            c0_two[i].wait_recv()
            c0_hand[i + 1].start()

    def c1_late():
        c1_two[0].wait_recv()
        c1_hand[1].start()
        arrive(c1_two[1:3])
        c1_hand[2].start()
        arrive(c1_two[3:5])
        c1_hand[3].start()

    by_core(c0_late, c1_late)

    arrive(c0_hand)
    arrive(w1)
    last = wr[3].reshape(256, 128)
    backward = []
    for a in (2, 1, 0):
        lines = jnp.concatenate(
            [wr[a].reshape(256, 128), last[:, 16 * a : 16 * a + 16]], axis=1
        )
        backward.append(lines.T)
    for plane in range(2):
        conv(backward, cg, plane)
        inp_ref[plane] = tap_sum(sums, -1, column).reshape(16, 8, 128).astype(jnp.bfloat16)

    arrive(a2)
    for half in range(2):
        lanes = pl.ds(pl.multiple_of(128 * sides[half], 128), 128)
        grad_ref[:, :, lanes] = full[half, 0:54].reshape(27, 16, 128)

    by_core(
        lambda: ended(v0_two + c0_one + c0_two + c0_hand),
        lambda: ended(v1_two + c1_one + c1_two + c1_hand),
    )
    ended(v_y + [v_x] + hand_one + hand_two + r_one + r_two + r_hand + sent)


def on_device(volume, kernel, cotangent):
    depth, chans, height, width = volume.shape
    nspace = lax.axis_size("space")
    scale = 1.0 / math.sqrt(depth * nspace * height * width)
    vmem = pl.BlockSpec(memory_space=pltpu.VMEM)
    bf16, f32 = jnp.bfloat16, jnp.float32
    return pl.pallas_call(
        functools.partial(layer_kernel, nspace, scale),
        out_shape=(
            jax.ShapeDtypeStruct(volume.shape, bf16),
            jax.ShapeDtypeStruct(volume.shape, bf16),
            jax.ShapeDtypeStruct((27, 16, 256), f32),
        ),
        in_specs=[vmem] * 3,
        out_specs=(vmem,) * 3,
        scratch_shapes=[
            pltpu.VMEM((2, 16, 1024), bf16),
            pltpu.VMEM((2, 16, 1024), bf16),
            pltpu.VMEM((2, 16, 1024), bf16),
            pltpu.VMEM((4, 2, 4, 2, 16, 1024), bf16),
            pltpu.VMEM((4, 2, 4, 2, 16, 1024), bf16),
            pltpu.VMEM((16, 4, 16, 128), bf16),
            pltpu.VMEM((4, 16, 16, 128), bf16),
            pltpu.VMEM((576, 1024), bf16),
            pltpu.VMEM((144, 1024), f32),
            pltpu.VMEM((2, 56, 8, 128), f32),
            pltpu.VMEM((2, 7, 7, 8, 128), f32),
            pltpu.VMEM((2, 2, 7, 8, 128), f32),
            pltpu.VMEM((2, 2, 7, 8, 128), f32),
            pltpu.VMEM((2, 7, 8, 128), f32),
            pltpu.VMEM((2, 56, 8, 128), f32),
            pltpu.SemaphoreType.DMA((COPIES,)),
            pltpu.SemaphoreType.DMA((COPIES,)),
            pltpu.SemaphoreType.REGULAR((2,)),
        ],
        compiler_params=pltpu.CompilerParams(
            collective_id=0, has_side_effects=True, vmem_limit_bytes=48 << 20
        ),
        name="layer",
    )(volume, cotangent, kernel)


def solution(mesh):
    return jax.shard_map(
        on_device,
        mesh=mesh,
        in_specs=(
            P("space", "chan", None, None),
            P(None, "chan", None),
            P("space", "chan", None, None),
        ),
        out_specs=(
            P("space", "chan", None, None),
            P("space", "chan", None, None),
            P(None, "chan", None),
        ),
        check_vma=False,
    )
```

```python
import functools
import math

import jax
import jax.numpy as jnp
from jax import lax
from jax.experimental import pallas as pl
from jax.experimental.pallas import tpu as pltpu
from jax.sharding import PartitionSpec as P

MESH = pl.DeviceIdType.MESH
COPIES = 112


def col_shift(x, step, column):
    if step == 0:
        return x
    width = x.shape[1]
    if step == 1:
        moved = pltpu.roll(x, width - 1, 1)
        return jnp.where(column == 127, 0.0, moved)
    moved = pltpu.roll(x, 1, 1)
    return jnp.where(column == 0, 0.0, moved)


def row_shift(x, step):
    if step == 0:
        return x
    zeros = jnp.zeros((x.shape[0], 128), x.dtype)
    if step == 1:
        return jnp.concatenate([x[:, 128:], zeros], axis=1)
    return jnp.concatenate([zeros, x[:, :-128]], axis=1)


def tap_sum(sums_ref, sign, column):
    total = None
    for b in range(3):
        line = None
        for c in range(3):
            tap = 3 * b + c
            part = col_shift(sums_ref[16 * tap : 16 * tap + 16, :], sign * (c - 1), column)
            line = part if line is None else line + part
        moved = row_shift(line, sign * (b - 1))
        total = moved if total is None else total + moved
    return total


def layer_kernel(
    nspace,
    scale,
    vol_ref,
    cot_ref,
    ker_ref,
    out_ref,
    inp_ref,
    grad_ref,
    rows,
    vol,
    cot,
    rim,
    vg,
    cg,
    kt,
    wr,
    cs,
    sums,
    part,
    near,
    quad,
    far,
    own,
    full,
    send_sem,
    recv_sem,
    known_sem,
):
    s = lax.axis_index("space")
    c = lax.axis_index("chan")
    nz = nspace // 2
    z, x_lo = s // 2, s % 2
    x_hi, y, core = c // 8, (c // 2) % 4, c % 2
    flip = (1 - x_hi) * 8 + y * 2 + core
    mate = c + 1 - 2 * core

    def at(dz, same):
        zz = lax.rem(z + dz + nz, nz)
        xx = x_lo if same else 1 - x_lo
        return zz * 2 + xx

    pair = at(0, False)
    edge = lax.rem(s + nspace + 2 * x_lo - 1, nspace)

    def y_at(dy):
        return lax.rem(y + dy, 4)

    def chan_of(dy):
        return x_hi * 8 + y_at(dy) * 2 + core

    peers = [(s, mate), (s, flip)] + [(s, chan_of(dy)) for dy in (1, 2, 3)]
    peers += [(pair, c), (pair, flip), (edge, c), (edge, flip)]
    peers += [(at(1, True), c), (at(-1, True), c)]
    barrier = pltpu.get_barrier_semaphore()
    for peer in peers:
        pl.semaphore_signal(barrier, inc=1, device_id=peer, device_id_type=MESH)

    for ref, flat in ((vol_ref, vol), (cot_ref, cot)):
        for plane in range(2):
            rows[plane] = ref[plane].astype(jnp.float32).reshape(128, 128)
            for h in range(8):
                line = rows[plane, pl.ds(h, 16, stride=8), :].astype(jnp.bfloat16)
                flat[plane, :, 128 * h : 128 * h + 128] = line
    pl.semaphore_wait(barrier, len(peers))

    count = [0]
    sent = []

    def copy_of(src, dst, peer, index=None):
        if index is None:
            index = count[0]
            count[0] += 1
        return pltpu.make_async_remote_copy(
            src_ref=src,
            dst_ref=dst,
            send_sem=send_sem.at[index],
            recv_sem=recv_sem.at[index],
            device_id=peer,
            device_id_type=MESH,
        )

    def send(src, dst, peer):
        copy = copy_of(src, dst, peer)
        copy.start()
        sent.append(copy)
        return copy

    def start(copies):
        for copy in copies:
            copy.start()

    def arrive(copies):
        for copy in copies:
            copy.wait_recv()

    def ended(copies):
        for copy in copies:
            copy.wait_send()

    def by_core(on_0, on_1):
        pl.when(core == 0)(on_0)
        pl.when(core == 1)(on_1)

    def tell(stage, dz):
        for step in (dz, -dz):
            pl.semaphore_signal(
                known_sem.at[stage], inc=1, device_id=(at(step, True), c), device_id_type=MESH
            )

    pair_src, pair_dst = 1 - x_lo, 2 + x_lo
    edge_src, edge_dst = x_lo, 3 - x_lo
    mine, rims = pl.ds(0, 2), pl.ds(2, 2)

    def hand(blocks, shared=None):
        return [
            copy_of(block, block, (s, mate), None if shared is None else shared[i])
            for i, block in enumerate(blocks)
        ]

    def to_y(src, dst):
        return [copy_of(src, dst, (s, chan_of(dy))) for dy in (1, 3, 2)]

    def to_rims(sources, targets):
        copies = [copy_of(sources[0], targets[0], (edge, to)) for to in (c, flip)]
        return copies + [copy_of(sources[1], targets[1], (pair, to)) for to in (c, flip)]

    def own_rims(block, g, lane):
        return to_rims(
            (block.at[edge_src], block.at[pair_src]),
            (g.at[edge_dst, x_hi, y, lane], g.at[pair_dst, x_hi, y, lane]),
        )

    def shared_sems():
        count[0] += 4
        return list(range(count[0] - 4, count[0]))

    own_block = vg.at[mine, x_hi, y, core]
    v_y = to_y(vol, own_block)
    v_x = copy_of(vol, own_block, (s, flip))
    start(v_y[0:2])
    v_x.start()
    v_y[2].start()
    r_one = own_rims(vol, vg, core)
    start(r_one)
    vg[0:2, x_hi, y, core] = vol[...]
    cg[0:2, x_hi, y, core] = cot[...]
    sides = (x_hi, 1 - x_hi)
    steps = (0, 3, 1, 2)
    hand_one = hand([vg.at[mine, sides[0], y_at(dy), core] for dy in steps])
    hand_two = hand([vg.at[mine, sides[1], y_at(dy), core] for dy in steps])
    sems = shared_sems()
    v0_two = [
        copy_of(
            vg.at[mine, sides[1], y, 0], vg.at[mine, sides[1], y, 0], (s, chan_of(dy)), sems[i]
        )
        for i, dy in enumerate((1, 3, 2))
    ]
    v1_two = [
        copy_of(
            vg.at[mine, sides[0], y_at(dy), 1],
            vg.at[mine, sides[0], y_at(dy), 1],
            (s, flip),
            sems[i],
        )
        for i, dy in enumerate((3, 1, 2))
    ]
    beside = [
        send(cot.at[edge_src], rim.at[edge_dst - 2], (edge, c)),
        send(cot.at[pair_src], rim.at[pair_dst - 2], (pair, c)),
    ]
    tell(0, 1)

    column = lax.broadcasted_iota(jnp.int32, (16, 1024), 1) % 128
    low = s == 0
    high = s == nspace - 1

    def spread(block, slot):
        for tap in range(9):
            b, cc = tap // 3, tap % 3
            moved = row_shift(col_shift(block, 1 - cc, column), 1 - b)
            first = 144 * slot + 16 * tap
            cs[first : first + 16, :] = moved.astype(jnp.bfloat16)

    for plane in range(2):
        spread(cot[plane].astype(jnp.float32), plane + 1)

    hand_one[0].start()
    v_x.wait_recv()
    pl.when(core == 0)(lambda: start(v0_two))
    hand_two[0].start()
    for i in range(3):
        v_y[i].wait_recv()
        pl.when(core == 1)(v1_two[i].start)
        hand_one[i + 1].start()
    pl.semaphore_wait(known_sem.at[0], 2)
    tell(1, 2)
    arrive(beside)
    below = rim[0].astype(jnp.float32)
    above = rim[1].astype(jnp.float32)
    spread(jnp.where(low, jnp.zeros_like(below), below), 0)
    spread(jnp.where(high, jnp.zeros_like(above), above), 3)

    pl.semaphore_wait(known_sem.at[1], 2)
    arrive(hand_one)

    def cell_dot(lhs, plane, half):
        return lax.dot_general(
            lhs,
            vg[plane, sides[half]].reshape(128, 1024),
            (((1,), (1,)), ((), ())),
            preferred_element_type=jnp.float32,
        )

    r = z % 4
    zi = z // 4
    held = pl.ds((x_lo * 4 + r) * 7, 7)
    moves = [(2, True), (-2, False), (1, True), (-1, True), (1, False), (-1, False), (0, False)]
    n1 = []

    def reduce_near(half):
        term = cell_dot(cs[0:432, :], 0, half) + cell_dot(cs[144:576, :], 1, half)
        for a in range(3):
            rows = term[144 * (2 - a) : 144 * (3 - a)]
            part[half, 18 * a : 18 * a + 18] = rows.reshape(18, 8, 128)
        part[half, 54:56] = jnp.zeros((2, 8, 128), jnp.float32)
        n1.append([])
        for slot, (dz, same) in enumerate(moves):
            group = (x_lo if same else 1 - x_lo) * 4 + (r + dz + 4) % 4
            n1[half].append(
                send(part.at[half, pl.ds(group * 7, 7)], near.at[half, slot], (at(dz, same), c))
            )

    reduce_near(0)

    for i in range(3):
        pl.when(core == 0)(v0_two[i].wait_recv)
        pl.when(core == 1)(v1_two[i].wait_recv)
        hand_two[i + 1].start()

    r_two = to_y(vg.at[rims, :, y, core], vg.at[rims, :, y, core])
    r_hand = hand([vg.at[rims, :, y_at(dy), core] for dy in (0, 3, 1, 2)])
    c0_one = [copy_of(cot, cg.at[mine, x_hi, y, 0], (s, flip))] + own_rims(cot, cg, 0)
    c0_two = to_y(cg.at[:, :, y, 0], cg.at[:, :, y, 0])
    c1_one = to_y(cot, cg.at[mine, x_hi, y, 1])
    c1_two = [copy_of(cg.at[mine, x_hi, :, 1], cg.at[mine, x_hi, :, 1], (s, flip))]
    c1_two += to_rims(
        (cg.at[edge_src, x_hi, :, 1], cg.at[pair_src, x_hi, :, 1]),
        (cg.at[edge_dst, x_hi, :, 1], cg.at[pair_dst, x_hi, :, 1]),
    )
    sems = shared_sems()
    c0_hand = hand([cg.at[:, :, y_at(dy), 0] for dy in (0, 3, 1, 2)], sems)
    c1_hand = hand(
        [
            cg.at[mine, x_hi, :, 1],
            cg.at[mine, 1 - x_hi, :, 1],
            cg.at[2 + x_lo, :, :, 1],
            cg.at[3 - x_lo, :, :, 1],
        ],
        sems,
    )
    arrive(hand_two)
    reduce_near(1)
    arrive(r_one)
    start(r_two)
    r_hand[0].start()
    by_core(lambda: start(c0_one), lambda: start(c1_one))

    hop = [at(4 * (1 - 2 * ((zi + r + i) % 2)), True) for i in range(2)]

    def exchange(half, step):
        return send(quad.at[half, step], far.at[half, step], (hop[(half + step) % 2], c))

    f1 = []
    for half in range(2):
        arrive(n1[half])
        total = part[half, held]
        for slot in range(7):
            total = total + near[half, slot]
        quad[half, 0] = total
        f1.append(exchange(half, 0))

    def c0_middle():
        arrive(c0_one)
        start(c0_two)
        c0_hand[0].start()

    def c1_middle():
        arrive(c1_one)
        start(c1_two)
        c1_hand[0].start()

    by_core(c0_middle, c1_middle)
    taps = [ker_ref[t].astype(jnp.float32) for t in range(27)]
    filler = jnp.zeros((16, 80), jnp.float32)
    for to in range(16):
        lanes = slice(16 * to, 16 * to + 16)
        for a in range(3):
            row = jnp.concatenate([taps[9 * a + t][:, lanes] for t in range(8)], axis=1)
            kt[to, a] = row.astype(jnp.bfloat16)
        row = jnp.concatenate([taps[9 * a + 8][:, lanes] for a in range(3)] + [filler], axis=1)
        kt[to, 3] = row.astype(jnp.bfloat16)
    wr[:, c] = kt[c]

    w1 = []
    for m in range(1, 16):
        to = lax.rem(c + m, 16)
        w1.append(send(kt.at[to], wr.at[:, c], (s, to)))

    def conv(weights, g, plane):
        order = (2, 0, 1) if plane == 0 else (0, 1, 3)
        total = None
        for taps_of, index in zip(weights, order):
            if index == 2:
                taps_of = jnp.where(low, jnp.zeros_like(taps_of), taps_of)
            if index == 3:
                taps_of = jnp.where(high, jnp.zeros_like(taps_of), taps_of)
            rows = g[index].reshape(256, 1024)
            product = jnp.dot(taps_of, rows, preferred_element_type=jnp.float32)
            total = product if total is None else total + product
        sums[...] = total

    f2 = []
    for half in range(2):
        f1[half].wait_recv()
        quad[half, 1] = quad[half, 0] + far[half, 0]
        f2.append(exchange(half, 1))

    a2 = []
    for half in range(2):
        f2[half].wait_recv()
        total = (quad[half, 1] + far[half, 1]) * scale
        own[half] = total
        full[half, held] = total
        for dz, same in moves:
            a2.append(send(own.at[half], full.at[half, held], (at(dz, same), c)))

    for i in range(3):
        r_two[i].wait_recv()
        r_hand[i + 1].start()
    arrive(r_hand)
    forward = [ker_ref[9 * a : 9 * a + 9].reshape(144, 256) for a in range(3)]
    for plane in range(2):
        conv(forward, vg, plane)
        out_ref[plane] = tap_sum(sums, 1, column).reshape(16, 8, 128).astype(jnp.bfloat16)

    def c0_late():
        for i in range(3):
            c0_two[i].wait_recv()
            c0_hand[i + 1].start()

    def c1_late():
        c1_two[0].wait_recv()
        c1_hand[1].start()
        arrive(c1_two[1:3])
        c1_hand[2].start()
        arrive(c1_two[3:5])
        c1_hand[3].start()

    by_core(c0_late, c1_late)

    arrive(c0_hand)
    arrive(w1)
    last = wr[3].reshape(256, 128)
    backward = []
    for a in (2, 1, 0):
        lines = jnp.concatenate(
            [wr[a].reshape(256, 128), last[:, 16 * a : 16 * a + 16]], axis=1
        )
        backward.append(lines.T)
    for plane in range(2):
        conv(backward, cg, plane)
        inp_ref[plane] = tap_sum(sums, -1, column).reshape(16, 8, 128).astype(jnp.bfloat16)

    arrive(a2)
    for half in range(2):
        lanes = pl.ds(pl.multiple_of(128 * sides[half], 128), 128)
        grad_ref[:, :, lanes] = full[half, 0:54].reshape(27, 16, 128)

    by_core(
        lambda: ended(v0_two + c0_one + c0_two + c0_hand),
        lambda: ended(v1_two + c1_one + c1_two + c1_hand),
    )
    ended(v_y + [v_x] + hand_one + hand_two + r_one + r_two + r_hand + sent)


def store_kernel(a_ref, b_ref, c_ref, a_out, b_out, c_out, sem):
    pairs = ((c_ref, c_out), (a_ref, a_out), (b_ref, b_out))
    copies = [pltpu.make_async_copy(x, y, sem.at[i]) for i, (x, y) in enumerate(pairs)]
    for copy in copies:
        copy.start()
    for copy in copies:
        copy.wait()


def on_device(volume, kernel, cotangent):
    depth, chans, height, width = volume.shape
    nspace = lax.axis_size("space")
    scale = 1.0 / math.sqrt(depth * nspace * height * width)
    vmem = pl.BlockSpec(memory_space=pltpu.VMEM)
    bf16, f32 = jnp.bfloat16, jnp.float32
    results = pl.pallas_call(
        functools.partial(layer_kernel, nspace, scale),
        out_shape=(
            jax.ShapeDtypeStruct(volume.shape, bf16),
            jax.ShapeDtypeStruct(volume.shape, bf16),
            jax.ShapeDtypeStruct((27, 16, 256), f32),
        ),
        in_specs=[vmem] * 3,
        out_specs=(vmem,) * 3,
        scratch_shapes=[
            pltpu.VMEM((2, 128, 128), f32),
            pltpu.VMEM((2, 16, 1024), bf16),
            pltpu.VMEM((2, 16, 1024), bf16),
            pltpu.VMEM((2, 16, 1024), bf16),
            pltpu.VMEM((4, 2, 4, 2, 16, 1024), bf16),
            pltpu.VMEM((4, 2, 4, 2, 16, 1024), bf16),
            pltpu.VMEM((16, 4, 16, 128), bf16),
            pltpu.VMEM((4, 16, 16, 128), bf16),
            pltpu.VMEM((576, 1024), bf16),
            pltpu.VMEM((144, 1024), f32),
            pltpu.VMEM((2, 56, 8, 128), f32),
            pltpu.VMEM((2, 7, 7, 8, 128), f32),
            pltpu.VMEM((2, 2, 7, 8, 128), f32),
            pltpu.VMEM((2, 2, 7, 8, 128), f32),
            pltpu.VMEM((2, 7, 8, 128), f32),
            pltpu.VMEM((2, 56, 8, 128), f32),
            pltpu.SemaphoreType.DMA((COPIES,)),
            pltpu.SemaphoreType.DMA((COPIES,)),
            pltpu.SemaphoreType.REGULAR((2,)),
        ],
        compiler_params=pltpu.CompilerParams(
            collective_id=0, has_side_effects=True, vmem_limit_bytes=48 << 20
        ),
        name="layer",
    )(volume, cotangent, kernel)
    return pl.pallas_call(
        store_kernel,
        out_shape=tuple(jax.ShapeDtypeStruct(x.shape, x.dtype) for x in results),
        in_specs=[vmem] * 3,
        out_specs=(pl.BlockSpec(memory_space=pltpu.HBM),) * 3,
        scratch_shapes=[pltpu.SemaphoreType.DMA((3,))],
        compiler_params=pltpu.CompilerParams(vmem_limit_bytes=8 << 20),
        name="store",
    )(*results)


def solution(mesh):
    return jax.shard_map(
        on_device,
        mesh=mesh,
        in_specs=(
            P("space", "chan", None, None),
            P(None, "chan", None),
            P("space", "chan", None, None),
        ),
        out_specs=(
            P("space", "chan", None, None),
            P("space", "chan", None, None),
            P(None, "chan", None),
        ),
        check_vma=False,
    )
```

```python
import functools
import math

import jax
import jax.numpy as jnp
from jax import lax
from jax.experimental import pallas as pl
from jax.experimental.pallas import tpu as pltpu
from jax.sharding import PartitionSpec as P

MESH = pl.DeviceIdType.MESH
COPIES = 112


def col_shift(x, step, column):
    if step == 0:
        return x
    width = x.shape[1]
    if step == 1:
        moved = pltpu.roll(x, width - 1, 1)
        return jnp.where(column == 127, 0.0, moved)
    moved = pltpu.roll(x, 1, 1)
    return jnp.where(column == 0, 0.0, moved)


def row_shift(x, step):
    if step == 0:
        return x
    zeros = jnp.zeros((x.shape[0], 128), x.dtype)
    if step == 1:
        return jnp.concatenate([x[:, 128:], zeros], axis=1)
    return jnp.concatenate([zeros, x[:, :-128]], axis=1)


def tap_sum(sums_ref, sign, column):
    total = None
    for b in range(3):
        line = None
        for c in range(3):
            tap = 3 * b + c
            part = col_shift(sums_ref[16 * tap : 16 * tap + 16, :], sign * (c - 1), column)
            line = part if line is None else line + part
        moved = row_shift(line, sign * (b - 1))
        total = moved if total is None else total + moved
    return total


def layer_kernel(
    nspace,
    scale,
    vol_ref,
    cot_ref,
    ker_ref,
    out_ref,
    inp_ref,
    grad_ref,
    rows,
    vol,
    cot,
    rim,
    vg,
    cg,
    kt,
    wr,
    cs,
    sums,
    part,
    near,
    quad,
    far,
    own,
    full,
    send_sem,
    recv_sem,
    known_sem,
):
    s = lax.axis_index("space")
    c = lax.axis_index("chan")
    nz = nspace // 2
    z, x_lo = s // 2, s % 2
    x_hi, y, core = c // 8, (c // 2) % 4, c % 2
    flip = (1 - x_hi) * 8 + y * 2 + core
    mate = c + 1 - 2 * core

    def at(dz, same):
        zz = lax.rem(z + dz + nz, nz)
        xx = x_lo if same else 1 - x_lo
        return zz * 2 + xx

    pair = at(0, False)
    edge = lax.rem(s + nspace + 2 * x_lo - 1, nspace)

    def y_at(dy):
        return lax.rem(y + dy, 4)

    def chan_of(dy):
        return x_hi * 8 + y_at(dy) * 2 + core

    peers = [(s, mate), (s, flip)] + [(s, chan_of(dy)) for dy in (1, 2, 3)]
    peers += [(pair, c), (pair, flip), (edge, c), (edge, flip)]
    peers += [(at(1, True), c), (at(-1, True), c)]
    barrier = pltpu.get_barrier_semaphore()
    for peer in peers:
        pl.semaphore_signal(barrier, inc=1, device_id=peer, device_id_type=MESH)

    for ref, flat in ((vol_ref, vol), (cot_ref, cot)):
        for plane in range(2):
            rows[plane] = ref[plane].astype(jnp.float32).reshape(128, 128)
            for h in range(8):
                line = rows[plane, pl.ds(h, 16, stride=8), :].astype(jnp.bfloat16)
                flat[plane, :, 128 * h : 128 * h + 128] = line
    pl.semaphore_wait(barrier, len(peers))

    count = [0]
    sent = []

    def copy_of(src, dst, peer, index=None):
        if index is None:
            index = count[0]
            count[0] += 1
        return pltpu.make_async_remote_copy(
            src_ref=src,
            dst_ref=dst,
            send_sem=send_sem.at[index],
            recv_sem=recv_sem.at[index],
            device_id=peer,
            device_id_type=MESH,
        )

    def send(src, dst, peer):
        copy = copy_of(src, dst, peer)
        copy.start()
        sent.append(copy)
        return copy

    def start(copies):
        for copy in copies:
            copy.start()

    def arrive(copies):
        for copy in copies:
            copy.wait_recv()

    def ended(copies):
        for copy in copies:
            copy.wait_send()

    def by_core(on_0, on_1):
        pl.when(core == 0)(on_0)
        pl.when(core == 1)(on_1)

    def tell(stage, dz):
        for step in (dz, -dz):
            pl.semaphore_signal(
                known_sem.at[stage], inc=1, device_id=(at(step, True), c), device_id_type=MESH
            )

    pair_src, pair_dst = 1 - x_lo, 2 + x_lo
    edge_src, edge_dst = x_lo, 3 - x_lo
    mine, rims = pl.ds(0, 2), pl.ds(2, 2)

    def hand(blocks, shared=None):
        return [
            copy_of(block, block, (s, mate), None if shared is None else shared[i])
            for i, block in enumerate(blocks)
        ]

    def to_y(src, dst):
        return [copy_of(src, dst, (s, chan_of(dy))) for dy in (1, 3, 2)]

    def to_rims(sources, targets):
        copies = [copy_of(sources[0], targets[0], (edge, to)) for to in (c, flip)]
        return copies + [copy_of(sources[1], targets[1], (pair, to)) for to in (c, flip)]

    def own_rims(block, g, lane):
        return to_rims(
            (block.at[edge_src], block.at[pair_src]),
            (g.at[edge_dst, x_hi, y, lane], g.at[pair_dst, x_hi, y, lane]),
        )

    def shared_sems():
        count[0] += 4
        return list(range(count[0] - 4, count[0]))

    own_block = vg.at[mine, x_hi, y, core]
    v_y = to_y(vol, own_block)
    v_x = copy_of(vol, own_block, (s, flip))
    start(v_y[0:2])
    v_x.start()
    v_y[2].start()
    vg[0:2, x_hi, y, core] = vol[...]
    cg[0:2, x_hi, y, core] = cot[...]
    sides = (x_hi, 1 - x_hi)
    steps = (0, 3, 1, 2)
    hand_one = hand([vg.at[mine, sides[0], y_at(dy), core] for dy in steps])
    hand_two = hand([vg.at[mine, sides[1], y_at(dy), core] for dy in steps])
    sems = shared_sems()
    v0_two = [
        copy_of(
            vg.at[mine, sides[1], y, 0], vg.at[mine, sides[1], y, 0], (s, chan_of(dy)), sems[i]
        )
        for i, dy in enumerate((1, 3, 2))
    ]
    v1_two = [
        copy_of(
            vg.at[mine, sides[0], y_at(dy), 1],
            vg.at[mine, sides[0], y_at(dy), 1],
            (s, flip),
            sems[i],
        )
        for i, dy in enumerate((3, 1, 2))
    ]
    beside = [
        send(cot.at[edge_src], rim.at[edge_dst - 2], (edge, c)),
        send(cot.at[pair_src], rim.at[pair_dst - 2], (pair, c)),
    ]
    tell(0, 1)

    column = lax.broadcasted_iota(jnp.int32, (16, 1024), 1) % 128
    low = s == 0
    high = s == nspace - 1

    def spread(block, slot):
        for tap in range(9):
            b, cc = tap // 3, tap % 3
            moved = row_shift(col_shift(block, 1 - cc, column), 1 - b)
            first = 144 * slot + 16 * tap
            cs[first : first + 16, :] = moved.astype(jnp.bfloat16)

    for plane in range(2):
        spread(cot[plane].astype(jnp.float32), plane + 1)

    hand_one[0].start()
    v_x.wait_recv()
    pl.when(core == 0)(lambda: start(v0_two))
    hand_two[0].start()
    for i in range(3):
        v_y[i].wait_recv()
        pl.when(core == 1)(v1_two[i].start)
        hand_one[i + 1].start()
    pl.semaphore_wait(known_sem.at[0], 2)
    tell(1, 2)
    arrive(beside)
    below = rim[0].astype(jnp.float32)
    above = rim[1].astype(jnp.float32)
    spread(jnp.where(low, jnp.zeros_like(below), below), 0)
    spread(jnp.where(high, jnp.zeros_like(above), above), 3)

    pl.semaphore_wait(known_sem.at[1], 2)
    arrive(hand_one)

    def cell_dot(lhs, plane, half):
        return lax.dot_general(
            lhs,
            vg[plane, sides[half]].reshape(128, 1024),
            (((1,), (1,)), ((), ())),
            preferred_element_type=jnp.float32,
        )

    r = z % 4
    zi = z // 4
    held = pl.ds((x_lo * 4 + r) * 7, 7)
    moves = [(2, True), (-2, False), (1, True), (-1, True), (1, False), (-1, False), (0, False)]
    n1 = []

    def reduce_near(half):
        term = cell_dot(cs[0:432, :], 0, half) + cell_dot(cs[144:576, :], 1, half)
        for a in range(3):
            rows = term[144 * (2 - a) : 144 * (3 - a)]
            part[half, 18 * a : 18 * a + 18] = rows.reshape(18, 8, 128)
        part[half, 54:56] = jnp.zeros((2, 8, 128), jnp.float32)
        n1.append([])
        for slot, (dz, same) in enumerate(moves):
            group = (x_lo if same else 1 - x_lo) * 4 + (r + dz + 4) % 4
            n1[half].append(
                send(part.at[half, pl.ds(group * 7, 7)], near.at[half, slot], (at(dz, same), c))
            )

    reduce_near(0)

    for i in range(3):
        pl.when(core == 0)(v0_two[i].wait_recv)
        pl.when(core == 1)(v1_two[i].wait_recv)
        hand_two[i + 1].start()

    r_one = own_rims(vol, vg, core)
    r_two = to_y(vg.at[rims, :, y, core], vg.at[rims, :, y, core])
    r_hand = hand([vg.at[rims, :, y_at(dy), core] for dy in (0, 3, 1, 2)])
    c0_one = [copy_of(cot, cg.at[mine, x_hi, y, 0], (s, flip))] + own_rims(cot, cg, 0)
    c0_two = to_y(cg.at[:, :, y, 0], cg.at[:, :, y, 0])
    c1_one = to_y(cot, cg.at[mine, x_hi, y, 1])
    c1_two = [copy_of(cg.at[mine, x_hi, :, 1], cg.at[mine, x_hi, :, 1], (s, flip))]
    c1_two += to_rims(
        (cg.at[edge_src, x_hi, :, 1], cg.at[pair_src, x_hi, :, 1]),
        (cg.at[edge_dst, x_hi, :, 1], cg.at[pair_dst, x_hi, :, 1]),
    )
    sems = shared_sems()
    c0_hand = hand([cg.at[:, :, y_at(dy), 0] for dy in (0, 3, 1, 2)], sems)
    c1_hand = hand(
        [
            cg.at[mine, x_hi, :, 1],
            cg.at[mine, 1 - x_hi, :, 1],
            cg.at[2 + x_lo, :, :, 1],
            cg.at[3 - x_lo, :, :, 1],
        ],
        sems,
    )
    start(r_one)
    by_core(lambda: start(c0_one), lambda: start(c1_one))
    arrive(hand_two)
    reduce_near(1)
    arrive(r_one)
    start(r_two)
    r_hand[0].start()

    hop = [at(4 * (1 - 2 * ((zi + r + i) % 2)), True) for i in range(2)]

    def exchange(half, step):
        return send(quad.at[half, step], far.at[half, step], (hop[(half + step) % 2], c))

    f1 = []
    for half in range(2):
        arrive(n1[half])
        total = part[half, held]
        for slot in range(7):
            total = total + near[half, slot]
        quad[half, 0] = total
        f1.append(exchange(half, 0))

    def c0_middle():
        arrive(c0_one)
        start(c0_two)
        c0_hand[0].start()

    def c1_middle():
        arrive(c1_one)
        start(c1_two)
        c1_hand[0].start()

    by_core(c0_middle, c1_middle)
    taps = [ker_ref[t].astype(jnp.float32) for t in range(27)]
    filler = jnp.zeros((16, 80), jnp.float32)
    for to in range(16):
        lanes = slice(16 * to, 16 * to + 16)
        for a in range(3):
            row = jnp.concatenate([taps[9 * a + t][:, lanes] for t in range(8)], axis=1)
            kt[to, a] = row.astype(jnp.bfloat16)
        row = jnp.concatenate([taps[9 * a + 8][:, lanes] for a in range(3)] + [filler], axis=1)
        kt[to, 3] = row.astype(jnp.bfloat16)
    wr[:, c] = kt[c]

    w1 = []
    for m in range(1, 16):
        to = lax.rem(c + m, 16)
        w1.append(send(kt.at[to], wr.at[:, c], (s, to)))

    def conv(weights, g, plane):
        order = (2, 0, 1) if plane == 0 else (0, 1, 3)
        total = None
        for taps_of, index in zip(weights, order):
            if index == 2:
                taps_of = jnp.where(low, jnp.zeros_like(taps_of), taps_of)
            if index == 3:
                taps_of = jnp.where(high, jnp.zeros_like(taps_of), taps_of)
            rows = g[index].reshape(256, 1024)
            product = jnp.dot(taps_of, rows, preferred_element_type=jnp.float32)
            total = product if total is None else total + product
        sums[...] = total

    f2 = []
    for half in range(2):
        f1[half].wait_recv()
        quad[half, 1] = quad[half, 0] + far[half, 0]
        f2.append(exchange(half, 1))

    a2 = []
    for half in range(2):
        f2[half].wait_recv()
        total = (quad[half, 1] + far[half, 1]) * scale
        own[half] = total
        full[half, held] = total
        for dz, same in moves:
            a2.append(send(own.at[half], full.at[half, held], (at(dz, same), c)))

    for i in range(3):
        r_two[i].wait_recv()
        r_hand[i + 1].start()
    arrive(r_hand)
    forward = [ker_ref[9 * a : 9 * a + 9].reshape(144, 256) for a in range(3)]
    for plane in range(2):
        conv(forward, vg, plane)
        out_ref[plane] = tap_sum(sums, 1, column).reshape(16, 8, 128).astype(jnp.bfloat16)

    def c0_late():
        for i in range(3):
            c0_two[i].wait_recv()
            c0_hand[i + 1].start()

    def c1_late():
        c1_two[0].wait_recv()
        c1_hand[1].start()
        arrive(c1_two[1:3])
        c1_hand[2].start()
        arrive(c1_two[3:5])
        c1_hand[3].start()

    by_core(c0_late, c1_late)

    arrive(c0_hand)
    arrive(w1)
    last = wr[3].reshape(256, 128)
    backward = []
    for a in (2, 1, 0):
        lines = jnp.concatenate(
            [wr[a].reshape(256, 128), last[:, 16 * a : 16 * a + 16]], axis=1
        )
        backward.append(lines.T)
    for plane in range(2):
        conv(backward, cg, plane)
        inp_ref[plane] = tap_sum(sums, -1, column).reshape(16, 8, 128).astype(jnp.bfloat16)

    arrive(a2)
    for half in range(2):
        lanes = pl.ds(pl.multiple_of(128 * sides[half], 128), 128)
        grad_ref[:, :, lanes] = full[half, 0:54].reshape(27, 16, 128)

    by_core(
        lambda: ended(v0_two + c0_one + c0_two + c0_hand),
        lambda: ended(v1_two + c1_one + c1_two + c1_hand),
    )
    ended(v_y + [v_x] + hand_one + hand_two + r_one + r_two + r_hand + sent)


def store_kernel(a_ref, b_ref, c_ref, a_out, b_out, c_out, sem):
    pairs = ((c_ref, c_out), (a_ref, a_out), (b_ref, b_out))
    copies = [pltpu.make_async_copy(x, y, sem.at[i]) for i, (x, y) in enumerate(pairs)]
    for copy in copies:
        copy.start()
    for copy in copies:
        copy.wait()


def on_device(volume, kernel, cotangent):
    depth, chans, height, width = volume.shape
    nspace = lax.axis_size("space")
    scale = 1.0 / math.sqrt(depth * nspace * height * width)
    vmem = pl.BlockSpec(memory_space=pltpu.VMEM)
    bf16, f32 = jnp.bfloat16, jnp.float32
    results = pl.pallas_call(
        functools.partial(layer_kernel, nspace, scale),
        out_shape=(
            jax.ShapeDtypeStruct(volume.shape, bf16),
            jax.ShapeDtypeStruct(volume.shape, bf16),
            jax.ShapeDtypeStruct((27, 16, 256), f32),
        ),
        in_specs=[vmem] * 3,
        out_specs=(vmem,) * 3,
        scratch_shapes=[
            pltpu.VMEM((2, 128, 128), f32),
            pltpu.VMEM((2, 16, 1024), bf16),
            pltpu.VMEM((2, 16, 1024), bf16),
            pltpu.VMEM((2, 16, 1024), bf16),
            pltpu.VMEM((4, 2, 4, 2, 16, 1024), bf16),
            pltpu.VMEM((4, 2, 4, 2, 16, 1024), bf16),
            pltpu.VMEM((16, 4, 16, 128), bf16),
            pltpu.VMEM((4, 16, 16, 128), bf16),
            pltpu.VMEM((576, 1024), bf16),
            pltpu.VMEM((144, 1024), f32),
            pltpu.VMEM((2, 56, 8, 128), f32),
            pltpu.VMEM((2, 7, 7, 8, 128), f32),
            pltpu.VMEM((2, 2, 7, 8, 128), f32),
            pltpu.VMEM((2, 2, 7, 8, 128), f32),
            pltpu.VMEM((2, 7, 8, 128), f32),
            pltpu.VMEM((2, 56, 8, 128), f32),
            pltpu.SemaphoreType.DMA((COPIES,)),
            pltpu.SemaphoreType.DMA((COPIES,)),
            pltpu.SemaphoreType.REGULAR((2,)),
        ],
        compiler_params=pltpu.CompilerParams(
            collective_id=0, has_side_effects=True, vmem_limit_bytes=48 << 20
        ),
        name="layer",
    )(volume, cotangent, kernel)
    return pl.pallas_call(
        store_kernel,
        out_shape=tuple(jax.ShapeDtypeStruct(x.shape, x.dtype) for x in results),
        in_specs=[vmem] * 3,
        out_specs=(pl.BlockSpec(memory_space=pltpu.HBM),) * 3,
        scratch_shapes=[pltpu.SemaphoreType.DMA((3,))],
        compiler_params=pltpu.CompilerParams(vmem_limit_bytes=8 << 20),
        name="store",
    )(*results)


def solution(mesh):
    return jax.shard_map(
        on_device,
        mesh=mesh,
        in_specs=(
            P("space", "chan", None, None),
            P(None, "chan", None),
            P("space", "chan", None, None),
        ),
        out_specs=(
            P("space", "chan", None, None),
            P("space", "chan", None, None),
            P(None, "chan", None),
        ),
        check_vma=False,
    )
```

```python
import functools
import math

import jax
import jax.numpy as jnp
from jax import lax
from jax.experimental import pallas as pl
from jax.experimental.pallas import tpu as pltpu
from jax.sharding import PartitionSpec as P

MESH = pl.DeviceIdType.MESH
COPIES = 112


def col_shift(x, step, column):
    if step == 0:
        return x
    width = x.shape[1]
    if step == 1:
        moved = pltpu.roll(x, width - 1, 1)
        return jnp.where(column == 127, 0.0, moved)
    moved = pltpu.roll(x, 1, 1)
    return jnp.where(column == 0, 0.0, moved)


def row_shift(x, step):
    if step == 0:
        return x
    zeros = jnp.zeros((x.shape[0], 128), x.dtype)
    if step == 1:
        return jnp.concatenate([x[:, 128:], zeros], axis=1)
    return jnp.concatenate([zeros, x[:, :-128]], axis=1)


def tap_sum(sums_ref, sign, column):
    total = None
    for b in range(3):
        line = None
        for c in range(3):
            tap = 3 * b + c
            part = col_shift(sums_ref[16 * tap : 16 * tap + 16, :], sign * (c - 1), column)
            line = part if line is None else line + part
        moved = row_shift(line, sign * (b - 1))
        total = moved if total is None else total + moved
    return total


def layer_kernel(
    nspace,
    scale,
    vol_hbm,
    cot_hbm,
    ker_hbm,
    out_ref,
    inp_ref,
    grad_ref,
    blocks,
    ker_ref,
    rows,
    vol,
    cot,
    rim,
    vg,
    cg,
    kt,
    wr,
    cs,
    sums,
    part,
    near,
    quad,
    far,
    own,
    full,
    send_sem,
    recv_sem,
    known_sem,
    load_sem,
):
    s = lax.axis_index("space")
    c = lax.axis_index("chan")
    nz = nspace // 2
    z, x_lo = s // 2, s % 2
    x_hi, y, core = c // 8, (c // 2) % 4, c % 2
    flip = (1 - x_hi) * 8 + y * 2 + core
    mate = c + 1 - 2 * core

    def at(dz, same):
        zz = lax.rem(z + dz + nz, nz)
        xx = x_lo if same else 1 - x_lo
        return zz * 2 + xx

    pair = at(0, False)
    edge = lax.rem(s + nspace + 2 * x_lo - 1, nspace)

    def y_at(dy):
        return lax.rem(y + dy, 4)

    def chan_of(dy):
        return x_hi * 8 + y_at(dy) * 2 + core

    peers = [(s, mate), (s, flip)] + [(s, chan_of(dy)) for dy in (1, 2, 3)]
    peers += [(pair, c), (pair, flip), (edge, c), (edge, flip)]
    peers += [(at(1, True), c), (at(-1, True), c)]
    barrier = pltpu.get_barrier_semaphore()
    for peer in peers:
        pl.semaphore_signal(barrier, inc=1, device_id=peer, device_id_type=MESH)

    loads = [
        pltpu.make_async_copy(vol_hbm, blocks.at[0], load_sem.at[0]),
        pltpu.make_async_copy(cot_hbm, blocks.at[1], load_sem.at[1]),
        pltpu.make_async_copy(ker_hbm, ker_ref, load_sem.at[2]),
    ]
    for load in loads:
        load.start()
    for k, flat in enumerate((vol, cot)):
        loads[k].wait()
        for plane in range(2):
            rows[plane] = blocks[k, plane].astype(jnp.float32).reshape(128, 128)
            for h in range(8):
                line = rows[plane, pl.ds(h, 16, stride=8), :].astype(jnp.bfloat16)
                flat[plane, :, 128 * h : 128 * h + 128] = line
    pl.semaphore_wait(barrier, len(peers))

    count = [0]
    sent = []

    def copy_of(src, dst, peer, index=None):
        if index is None:
            index = count[0]
            count[0] += 1
        return pltpu.make_async_remote_copy(
            src_ref=src,
            dst_ref=dst,
            send_sem=send_sem.at[index],
            recv_sem=recv_sem.at[index],
            device_id=peer,
            device_id_type=MESH,
        )

    def send(src, dst, peer):
        copy = copy_of(src, dst, peer)
        copy.start()
        sent.append(copy)
        return copy

    def start(copies):
        for copy in copies:
            copy.start()

    def arrive(copies):
        for copy in copies:
            copy.wait_recv()

    def ended(copies):
        for copy in copies:
            copy.wait_send()

    def by_core(on_0, on_1):
        pl.when(core == 0)(on_0)
        pl.when(core == 1)(on_1)

    def tell(stage, dz):
        for step in (dz, -dz):
            pl.semaphore_signal(
                known_sem.at[stage], inc=1, device_id=(at(step, True), c), device_id_type=MESH
            )

    pair_src, pair_dst = 1 - x_lo, 2 + x_lo
    edge_src, edge_dst = x_lo, 3 - x_lo
    mine, rims = pl.ds(0, 2), pl.ds(2, 2)

    def hand(blocks, shared=None):
        return [
            copy_of(block, block, (s, mate), None if shared is None else shared[i])
            for i, block in enumerate(blocks)
        ]

    def to_y(src, dst):
        return [copy_of(src, dst, (s, chan_of(dy))) for dy in (1, 3, 2)]

    def to_rims(sources, targets):
        copies = [copy_of(sources[0], targets[0], (edge, to)) for to in (c, flip)]
        return copies + [copy_of(sources[1], targets[1], (pair, to)) for to in (c, flip)]

    def own_rims(block, g, lane):
        return to_rims(
            (block.at[edge_src], block.at[pair_src]),
            (g.at[edge_dst, x_hi, y, lane], g.at[pair_dst, x_hi, y, lane]),
        )

    def shared_sems():
        count[0] += 4
        return list(range(count[0] - 4, count[0]))

    own_block = vg.at[mine, x_hi, y, core]
    v_y = to_y(vol, own_block)
    v_x = copy_of(vol, own_block, (s, flip))
    start(v_y[0:2])
    v_x.start()
    v_y[2].start()
    vg[0:2, x_hi, y, core] = vol[...]
    cg[0:2, x_hi, y, core] = cot[...]
    sides = (x_hi, 1 - x_hi)
    steps = (0, 3, 1, 2)
    hand_one = hand([vg.at[mine, sides[0], y_at(dy), core] for dy in steps])
    hand_two = hand([vg.at[mine, sides[1], y_at(dy), core] for dy in steps])
    sems = shared_sems()
    v0_two = [
        copy_of(
            vg.at[mine, sides[1], y, 0], vg.at[mine, sides[1], y, 0], (s, chan_of(dy)), sems[i]
        )
        for i, dy in enumerate((1, 3, 2))
    ]
    v1_two = [
        copy_of(
            vg.at[mine, sides[0], y_at(dy), 1],
            vg.at[mine, sides[0], y_at(dy), 1],
            (s, flip),
            sems[i],
        )
        for i, dy in enumerate((3, 1, 2))
    ]
    beside = [
        send(cot.at[edge_src], rim.at[edge_dst - 2], (edge, c)),
        send(cot.at[pair_src], rim.at[pair_dst - 2], (pair, c)),
    ]
    tell(0, 1)

    column = lax.broadcasted_iota(jnp.int32, (16, 1024), 1) % 128
    low = s == 0
    high = s == nspace - 1

    def spread(block, slot):
        for tap in range(9):
            b, cc = tap // 3, tap % 3
            moved = row_shift(col_shift(block, 1 - cc, column), 1 - b)
            first = 144 * slot + 16 * tap
            cs[first : first + 16, :] = moved.astype(jnp.bfloat16)

    for plane in range(2):
        spread(cot[plane].astype(jnp.float32), plane + 1)

    hand_one[0].start()
    v_x.wait_recv()
    pl.when(core == 0)(lambda: start(v0_two))
    hand_two[0].start()
    for i in range(3):
        v_y[i].wait_recv()
        pl.when(core == 1)(v1_two[i].start)
        hand_one[i + 1].start()
    pl.semaphore_wait(known_sem.at[0], 2)
    tell(1, 2)
    arrive(beside)
    below = rim[0].astype(jnp.float32)
    above = rim[1].astype(jnp.float32)
    spread(jnp.where(low, jnp.zeros_like(below), below), 0)
    spread(jnp.where(high, jnp.zeros_like(above), above), 3)

    pl.semaphore_wait(known_sem.at[1], 2)
    arrive(hand_one)

    def cell_dot(lhs, plane, half):
        return lax.dot_general(
            lhs,
            vg[plane, sides[half]].reshape(128, 1024),
            (((1,), (1,)), ((), ())),
            preferred_element_type=jnp.float32,
        )

    r = z % 4
    zi = z // 4
    held = pl.ds((x_lo * 4 + r) * 7, 7)
    moves = [(2, True), (-2, False), (1, True), (-1, True), (1, False), (-1, False), (0, False)]
    n1 = []

    def reduce_near(half):
        term = cell_dot(cs[0:432, :], 0, half) + cell_dot(cs[144:576, :], 1, half)
        for a in range(3):
            rows = term[144 * (2 - a) : 144 * (3 - a)]
            part[half, 18 * a : 18 * a + 18] = rows.reshape(18, 8, 128)
        part[half, 54:56] = jnp.zeros((2, 8, 128), jnp.float32)
        n1.append([])
        for slot, (dz, same) in enumerate(moves):
            group = (x_lo if same else 1 - x_lo) * 4 + (r + dz + 4) % 4
            n1[half].append(
                send(part.at[half, pl.ds(group * 7, 7)], near.at[half, slot], (at(dz, same), c))
            )

    reduce_near(0)

    for i in range(3):
        pl.when(core == 0)(v0_two[i].wait_recv)
        pl.when(core == 1)(v1_two[i].wait_recv)
        hand_two[i + 1].start()

    r_one = own_rims(vol, vg, core)
    r_two = to_y(vg.at[rims, :, y, core], vg.at[rims, :, y, core])
    r_hand = hand([vg.at[rims, :, y_at(dy), core] for dy in (0, 3, 1, 2)])
    c0_one = [copy_of(cot, cg.at[mine, x_hi, y, 0], (s, flip))] + own_rims(cot, cg, 0)
    c0_two = to_y(cg.at[:, :, y, 0], cg.at[:, :, y, 0])
    c1_one = to_y(cot, cg.at[mine, x_hi, y, 1])
    c1_two = [copy_of(cg.at[mine, x_hi, :, 1], cg.at[mine, x_hi, :, 1], (s, flip))]
    c1_two += to_rims(
        (cg.at[edge_src, x_hi, :, 1], cg.at[pair_src, x_hi, :, 1]),
        (cg.at[edge_dst, x_hi, :, 1], cg.at[pair_dst, x_hi, :, 1]),
    )
    sems = shared_sems()
    c0_hand = hand([cg.at[:, :, y_at(dy), 0] for dy in (0, 3, 1, 2)], sems)
    c1_hand = hand(
        [
            cg.at[mine, x_hi, :, 1],
            cg.at[mine, 1 - x_hi, :, 1],
            cg.at[2 + x_lo, :, :, 1],
            cg.at[3 - x_lo, :, :, 1],
        ],
        sems,
    )
    start(r_one)
    by_core(lambda: start(c0_one), lambda: start(c1_one))
    arrive(hand_two)
    reduce_near(1)
    arrive(r_one)
    start(r_two)
    r_hand[0].start()

    hop = [at(4 * (1 - 2 * ((zi + r + i) % 2)), True) for i in range(2)]

    def exchange(half, step):
        return send(quad.at[half, step], far.at[half, step], (hop[(half + step) % 2], c))

    f1 = []
    for half in range(2):
        arrive(n1[half])
        total = part[half, held]
        for slot in range(7):
            total = total + near[half, slot]
        quad[half, 0] = total
        f1.append(exchange(half, 0))

    def c0_middle():
        arrive(c0_one)
        start(c0_two)
        c0_hand[0].start()

    def c1_middle():
        arrive(c1_one)
        start(c1_two)
        c1_hand[0].start()

    by_core(c0_middle, c1_middle)
    loads[2].wait()
    taps = [ker_ref[t].astype(jnp.float32) for t in range(27)]
    filler = jnp.zeros((16, 80), jnp.float32)
    for to in range(16):
        lanes = slice(16 * to, 16 * to + 16)
        for a in range(3):
            row = jnp.concatenate([taps[9 * a + t][:, lanes] for t in range(8)], axis=1)
            kt[to, a] = row.astype(jnp.bfloat16)
        row = jnp.concatenate([taps[9 * a + 8][:, lanes] for a in range(3)] + [filler], axis=1)
        kt[to, 3] = row.astype(jnp.bfloat16)
    wr[:, c] = kt[c]

    w1 = []
    for m in range(1, 16):
        to = lax.rem(c + m, 16)
        w1.append(send(kt.at[to], wr.at[:, c], (s, to)))

    def conv(weights, g, plane):
        order = (2, 0, 1) if plane == 0 else (0, 1, 3)
        total = None
        for taps_of, index in zip(weights, order):
            if index == 2:
                taps_of = jnp.where(low, jnp.zeros_like(taps_of), taps_of)
            if index == 3:
                taps_of = jnp.where(high, jnp.zeros_like(taps_of), taps_of)
            rows = g[index].reshape(256, 1024)
            product = jnp.dot(taps_of, rows, preferred_element_type=jnp.float32)
            total = product if total is None else total + product
        sums[...] = total

    f2 = []
    for half in range(2):
        f1[half].wait_recv()
        quad[half, 1] = quad[half, 0] + far[half, 0]
        f2.append(exchange(half, 1))

    a2 = []
    for half in range(2):
        f2[half].wait_recv()
        total = (quad[half, 1] + far[half, 1]) * scale
        own[half] = total
        full[half, held] = total
        for dz, same in moves:
            a2.append(send(own.at[half], full.at[half, held], (at(dz, same), c)))

    for i in range(3):
        r_two[i].wait_recv()
        r_hand[i + 1].start()
    arrive(r_hand)
    forward = [ker_ref[9 * a : 9 * a + 9].reshape(144, 256) for a in range(3)]
    for plane in range(2):
        conv(forward, vg, plane)
        out_ref[plane] = tap_sum(sums, 1, column).reshape(16, 8, 128).astype(jnp.bfloat16)

    def c0_late():
        for i in range(3):
            c0_two[i].wait_recv()
            c0_hand[i + 1].start()

    def c1_late():
        c1_two[0].wait_recv()
        c1_hand[1].start()
        arrive(c1_two[1:3])
        c1_hand[2].start()
        arrive(c1_two[3:5])
        c1_hand[3].start()

    by_core(c0_late, c1_late)

    arrive(c0_hand)
    arrive(w1)
    last = wr[3].reshape(256, 128)
    backward = []
    for a in (2, 1, 0):
        lines = jnp.concatenate(
            [wr[a].reshape(256, 128), last[:, 16 * a : 16 * a + 16]], axis=1
        )
        backward.append(lines.T)
    for plane in range(2):
        conv(backward, cg, plane)
        inp_ref[plane] = tap_sum(sums, -1, column).reshape(16, 8, 128).astype(jnp.bfloat16)

    arrive(a2)
    for half in range(2):
        lanes = pl.ds(pl.multiple_of(128 * sides[half], 128), 128)
        grad_ref[:, :, lanes] = full[half, 0:54].reshape(27, 16, 128)

    by_core(
        lambda: ended(v0_two + c0_one + c0_two + c0_hand),
        lambda: ended(v1_two + c1_one + c1_two + c1_hand),
    )
    ended(v_y + [v_x] + hand_one + hand_two + r_one + r_two + r_hand + sent)


def store_kernel(a_ref, b_ref, c_ref, a_out, b_out, c_out, a, b, c, sem):
    parts = ((c_ref, c, c_out), (a_ref, a, a_out), (b_ref, b, b_out))
    loads = [pltpu.make_async_copy(x, v, sem.at[i]) for i, (x, v, y) in enumerate(parts)]
    stores = [pltpu.make_async_copy(v, y, sem.at[i + 3]) for i, (x, v, y) in enumerate(parts)]
    for load in loads:
        load.start()
    for load, store in zip(loads, stores):
        load.wait()
        store.start()
    for store in stores:
        store.wait()


def on_device(volume, kernel, cotangent):
    depth, chans, height, width = volume.shape
    nspace = lax.axis_size("space")
    scale = 1.0 / math.sqrt(depth * nspace * height * width)
    vmem = pl.BlockSpec(memory_space=pltpu.VMEM)
    bf16, f32 = jnp.bfloat16, jnp.float32
    results = pl.pallas_call(
        functools.partial(layer_kernel, nspace, scale),
        out_shape=(
            jax.ShapeDtypeStruct(volume.shape, bf16),
            jax.ShapeDtypeStruct(volume.shape, bf16),
            jax.ShapeDtypeStruct((27, 16, 256), f32),
        ),
        in_specs=[pl.BlockSpec(memory_space=pltpu.HBM)] * 3,
        out_specs=(vmem,) * 3,
        scratch_shapes=[
            pltpu.VMEM((2, 2, 16, 8, 128), bf16),
            pltpu.VMEM((27, 16, 256), bf16),
            pltpu.VMEM((2, 128, 128), f32),
            pltpu.VMEM((2, 16, 1024), bf16),
            pltpu.VMEM((2, 16, 1024), bf16),
            pltpu.VMEM((2, 16, 1024), bf16),
            pltpu.VMEM((4, 2, 4, 2, 16, 1024), bf16),
            pltpu.VMEM((4, 2, 4, 2, 16, 1024), bf16),
            pltpu.VMEM((16, 4, 16, 128), bf16),
            pltpu.VMEM((4, 16, 16, 128), bf16),
            pltpu.VMEM((576, 1024), bf16),
            pltpu.VMEM((144, 1024), f32),
            pltpu.VMEM((2, 56, 8, 128), f32),
            pltpu.VMEM((2, 7, 7, 8, 128), f32),
            pltpu.VMEM((2, 2, 7, 8, 128), f32),
            pltpu.VMEM((2, 2, 7, 8, 128), f32),
            pltpu.VMEM((2, 7, 8, 128), f32),
            pltpu.VMEM((2, 56, 8, 128), f32),
            pltpu.SemaphoreType.DMA((COPIES,)),
            pltpu.SemaphoreType.DMA((COPIES,)),
            pltpu.SemaphoreType.REGULAR((2,)),
            pltpu.SemaphoreType.DMA((3,)),
        ],
        compiler_params=pltpu.CompilerParams(
            collective_id=0, has_side_effects=True, vmem_limit_bytes=61 << 20
        ),
        name="layer",
    )(volume, cotangent, kernel)
    return pl.pallas_call(
        store_kernel,
        out_shape=tuple(jax.ShapeDtypeStruct(x.shape, x.dtype) for x in results),
        in_specs=[pl.BlockSpec(memory_space=pltpu.HBM)] * 3,
        out_specs=(pl.BlockSpec(memory_space=pltpu.HBM),) * 3,
        scratch_shapes=[pltpu.VMEM(x.shape, x.dtype) for x in results]
        + [pltpu.SemaphoreType.DMA((6,))],
        compiler_params=pltpu.CompilerParams(vmem_limit_bytes=61 << 20),
        name="store",
    )(*results)


def solution(mesh):
    return jax.shard_map(
        on_device,
        mesh=mesh,
        in_specs=(
            P("space", "chan", None, None),
            P(None, "chan", None),
            P("space", "chan", None, None),
        ),
        out_specs=(
            P("space", "chan", None, None),
            P("space", "chan", None, None),
            P(None, "chan", None),
        ),
        check_vma=False,
    )
```
